128 devices in a mesh: row: 16 (over y, x_lo, core), col: 8 (over x_hi, z).
Axes of the slice: x: 4 (x_hi: 2, x_lo: 2; x = x_hi * 2 + x_lo), y: 4, z: 4, core: 2. Of those that a mesh axis runs over, the one named last changes fastest.
Arguments:
- amplitudes: float32 [512, 32, 32, 32], P('col', 'row'), may hold values from -6 to 6
- integrals: float32 [1024, 16384], P('col', 'row'), may hold values from -0.1875 to 0.1875
- occ_energy: float32 [32], replicated, may hold values from -2 to -0.5
- vir_energy: float32 [512], replicated, may hold values from 0.3 to 3
Outputs:
- residual: float32 [16384, 16384], P('col', 'row')
The draws below stay inside these ranges and needn't reach their ends.
All inputs are finite; a program needn't handle non-finite values.
Results may differ from the reference program's by a relative error of at most 0.00007.
Values sent between devices are 32-bit elements; how exact they have to be, the bound alone decides.
No kernel may reach another device: no remote copies, remote signals or barrier semaphores. Data moves between devices by JAX's collectives and lax.ppermute only.
A program may use at most 128 MiB of HBM per device.

```python
import jax
import jax.numpy as jnp
from jax import lax

V = 512
O = 32
KWIN = 1024
NOV = 16384
CWIN = 32


def block_scale(own_key, shape, cuts, least, high):
    factor_of = 1.0
    for dim, parts in cuts:
        steps = jax.random.uniform(jax.random.fold_in(jax.random.fold_in(own_key, 6), dim), (parts,), jnp.float32, least / len(cuts), high / len(cuts))
        factor_of = factor_of * jnp.repeat(jnp.exp(steps), shape[dim] // parts).reshape((-1,) + (1,) * (len(shape) - 1 - dim))
    return factor_of


def gaussian(key, dims, spread, most, cuts=(), dtype=jnp.bfloat16):
    result = spread * jax.random.normal(key, dims, jnp.float32)
    if cuts:
        result = result * block_scale(key, dims, cuts, -0.22, 0.18)
    return jnp.clip(result, -most, most).astype(dtype)


def setup_inputs(seed: int = 0) -> dict:
    arg_keys = jax.random.split(jax.random.key(seed), 5)
    amplitudes = gaussian(arg_keys[0], (V, O, CWIN, O), 1.0, 6.0, ((0, 8), (1, 16)), jnp.float32)
    integrals = gaussian(arg_keys[1], (KWIN, NOV), KWIN ** -0.5, 0.1875, ((0, 8), (1, 16)), jnp.float32)
    occ_energy = jnp.clip(jax.random.uniform(arg_keys[2], (O,), jnp.float32, -2.0, -0.5), -2.0, -0.5)
    vir_energy = jnp.clip(jax.random.uniform(arg_keys[3], (V,), jnp.float32, 0.3, 3.0), 0.3, 3.0)
    return {"amplitudes": amplitudes, "integrals": integrals, "occ_energy": occ_energy, "vir_energy": vir_energy}


def reference(amplitudes, integrals, occ_energy, vir_energy):
    amp_matrix = amplitudes.reshape(V * O, KWIN)
    contracted = jnp.dot(amp_matrix, integrals, preferred_element_type=jnp.float32, precision=lax.Precision.HIGHEST)
    gap = (vir_energy[:, None] - occ_energy[None, :]).reshape(V * O)
    return contracted / (gap[:, None] + gap[None, :])
```

```python
import functools

import jax
import jax.numpy as jnp
import numpy as np
from jax import lax
from jax.experimental import pallas as pl
from jax.experimental.pallas import tpu as pltpu
from jax.sharding import Mesh, PartitionSpec as P

ROW = ("y", "xl", "core")
COL = ("xh", "z")
AXES = ROW + COL
SIZES = (4, 2, 2, 2, 4)
f32, bf16 = jnp.float32, jnp.bfloat16
MIB = 1 << 20


def hop(value, **move):
    pairs = []
    for source in range(int(np.prod(SIZES))):
        place = list(np.unravel_index(source, SIZES))
        for axis, step in move.items():
            k = AXES.index(axis)
            place[k] = (place[k] + step) % SIZES[k]
        pairs.append((source, int(np.ravel_multi_index(place, SIZES))))
    return lax.ppermute(value, AXES, pairs)


def after(value, *needed):
    return lax.optimization_barrier((value,) + needed)[0]


def split(value):
    high = value.astype(bf16)
    return high, (value - high.astype(f32)).astype(bf16)


def turn_kernel(amp_ref, out_ref):
    for n in range(out_ref.shape[0]):
        lanes = slice(n * 128, n * 128 + 128)
        both = jnp.concatenate([amp_ref[0, lanes], amp_ref[1, lanes]], axis=1)
        out_ref[n] = both.T


def turn(amp):
    two, depth, width = amp.shape
    return pl.pallas_call(
        turn_kernel,
        out_shape=jax.ShapeDtypeStruct((depth // 128, two * width, 128), f32),
        in_specs=[pl.BlockSpec(memory_space=pltpu.VMEM)],
        out_specs=pl.BlockSpec(memory_space=pltpu.VMEM),
        name="turn",
    )(amp)


def prep_kernel(pieces, slots_ref, *refs):
    sources, (high_ref, low_ref), (held, sem) = refs[: len(pieces)], refs[len(pieces) : len(pieces) + 2], refs[len(pieces) + 2 :]
    copies = []
    number = 0
    for ref, parts in zip(sources, pieces):
        for start, rows, slot, offset in parts:
            row = pl.multiple_of(slots_ref[slot] * 128 + offset, 8)
            copies.append(pltpu.make_async_copy(ref.at[:, pl.ds(start, rows)], held.at[:, pl.ds(row, rows)], sem.at[number]))
            number += 1
    for copy in copies:
        copy.start()
    for copy in copies:
        copy.wait()
    width = held.shape[1] // 8
    for n in range(held.shape[0]):
        lane = n * 128
        for a in range(0, width, 2):
            value = jnp.concatenate(
                [held[n, pl.ds(a + b, 8, stride=width), :] for b in range(2)], axis=0
            )
            high, low = split(value)
            high_ref[a * 8 : a * 8 + 16, lane : lane + 128] = high
            low_ref[a * 8 : a * 8 + 16, lane : lane + 128] = low


def prep(slots, sources, pieces):
    depth = sources[0].shape[0] * 128
    rows = 4 * sources[0].shape[1]
    count = sum(len(p) for p in pieces)
    return pl.pallas_call(
        functools.partial(prep_kernel, pieces),
        out_shape=[jax.ShapeDtypeStruct((rows, depth), bf16)] * 2,
        in_specs=[pl.BlockSpec(memory_space=pltpu.SMEM)] + [pl.BlockSpec(memory_space=pl.ANY)] * len(sources),
        out_specs=[pl.BlockSpec(memory_space=pltpu.VMEM)] * 2,
        scratch_shapes=[pltpu.VMEM((depth // 128, rows, 128), f32), pltpu.SemaphoreType.DMA((count,))],
        cost_estimate=pl.CostEstimate(flops=rows * depth * 4, bytes_accessed=rows * depth * 8, transcendentals=0),
        name="prep",
    )(slots, *sources)


def prep_w_kernel(slots_ref, *refs):
    sources, (high_ref, low_ref), (held, sem) = refs[:8], refs[8:10], refs[10:]
    copies = [
        pltpu.make_async_copy(ref, held.at[slots_ref[n]], sem.at[n]) for n, ref in enumerate(sources)
    ]
    for copy in copies:
        copy.start()
    for copy in copies:
        copy.wait()
    for n in range(8):
        high, low = split(held[n])
        high_ref[n] = high
        low_ref[n] = low


def prep_w(slots, sources):
    rows, columns = sources[0].shape
    return pl.pallas_call(
        prep_w_kernel,
        out_shape=[jax.ShapeDtypeStruct((8, rows, columns), bf16)] * 2,
        in_specs=[pl.BlockSpec(memory_space=pltpu.SMEM)] + [pl.BlockSpec(memory_space=pl.ANY)] * 8,
        out_specs=[pl.BlockSpec(memory_space=pltpu.VMEM)] * 2,
        scratch_shapes=[pltpu.VMEM((8, rows, columns), f32), pltpu.SemaphoreType.DMA((8,))],
        name="prep_w",
    )(slots, *sources)


def mm_kernel(ys_ref, *refs):
    (*a_refs, whigh_ref, wlow_ref, rgap_ref, cgap_ref, out_ref) = refs
    chunk = pl.program_id(0)
    depth, columns = whigh_ref.shape

    def work(high_ref, low_ref):
        high, low = high_ref[...], low_ref[...]
        tall = rgap_ref[...].reshape(-1, 128)
        for n in range(0, columns, 256):
            wh, wl = whigh_ref[:, n : n + 256], wlow_ref[:, n : n + 256]
            total = jnp.dot(high, wh, preferred_element_type=f32)
            total += jnp.dot(high, wl, preferred_element_type=f32)
            total += jnp.dot(low, wh, preferred_element_type=f32)
            for m in range(0, 256, 128):
                gap = tall + cgap_ref[:, n + m : n + m + 128]
                out_ref[:, 0, :, n + m : n + m + 128] = (total[:, m : m + 128] / gap).reshape(-1, 8, 128)

    for j in range(4):
        pl.when(chunk == j)(functools.partial(work, a_refs[2 * j], a_refs[2 * j + 1]))


def matmul(ys, parts, whigh, wlow, rgap, cgap, virtuals):
    depth, columns = whigh.shape
    steps = 2
    rows = parts[0].shape[0] // steps

    def a_spec(j):
        return pl.BlockSpec(
            (rows, depth), lambda c, s, ys: (jnp.where(c == j, s, jnp.where(c < j, 0, steps - 1)), 0)
        )

    return pl.pallas_call(
        mm_kernel,
        out_shape=jax.ShapeDtypeStruct((virtuals, 4, 8, columns), f32),
        grid_spec=pltpu.PrefetchScalarGridSpec(
            num_scalar_prefetch=1,
            grid=(4, steps),
            in_specs=[a_spec(j // 2) for j in range(8)]
            + [
                pl.BlockSpec((depth, columns), lambda c, s, ys: (0, 0)),
                pl.BlockSpec((depth, columns), lambda c, s, ys: (0, 0)),
                pl.BlockSpec((virtuals // steps, 1, 8, 128), lambda c, s, ys: (s, ys[c], 0, 0)),
                pl.BlockSpec((1, columns), lambda c, s, ys: (0, 0)),
            ],
            out_specs=pl.BlockSpec((virtuals // steps, 1, 8, columns), lambda c, s, ys: (s, ys[c], 0, 0)),
        ),
        compiler_params=pltpu.CompilerParams(vmem_limit_bytes=40 * MIB),
        name="contract",
    )(ys, *parts, whigh, wlow, rgap, cgap)


def body(amplitudes, integrals, occ_energy, vir_energy):
    virtuals, own = amplitudes.shape[:2]
    depth = amplitudes.shape[2] * amplitudes.shape[3]
    columns = integrals.shape[1]
    y, xl, core, xh, z = (lax.axis_index(a) for a in AXES)

    x = turn(amplitudes.transpose(1, 2, 3, 0).reshape(own, depth, virtuals))
    w = integrals
    half = x.shape[1] // 2

    wp, wm = hop(w, z=1), hop(w, z=3)
    xp, xm, xx = hop(x, y=1), hop(x, y=3), hop(x, xl=1)
    xxp, xxm = hop(xx, y=1), hop(xx, y=3)
    w2, wx = hop(after(w, wp), z=2), hop(after(w, xx), xh=1)
    c0 = [hop(x, core=1), hop(xx, core=1)]
    c1 = [hop(xp, core=1), hop(xxp, core=1)]
    c2 = [hop(xm, core=1), hop(xxm, core=1)]
    up = hop(jnp.concatenate([xp[:, :half], xxp[:, :half]], axis=1), y=1)
    down = hop(jnp.concatenate([xm[:, half:], xxm[:, half:]], axis=1), y=3)
    wxp, wxm, wx2 = hop(wx, z=1), hop(wx, z=3), hop(w2, xh=1)
    c3 = [hop(up, core=1), hop(down, core=1)]

    slots = jnp.stack([xl * 2 + core, (1 - xl) * 2 + core, xl * 2 + 1 - core, (1 - xl) * 2 + 1 - core]).astype(jnp.int32)
    rows = 2 * half
    whole = [((0, rows, n, 0),) for n in range(4)]
    up_parts = lambda n: ((0, half, n, 0), (half, half, n + 1, 0))
    down_parts = lambda n: ((0, half, n, half), (half, half, n + 1, half))
    parts = []
    parts += prep(slots, [x, xx, *c0], whole)
    parts += prep(slots, [xp, xxp, *c1], whole)
    parts += prep(slots, [xm, xxm, *c2], whole)
    parts += prep(slots, [up, down, *c3], [up_parts(0), down_parts(0), up_parts(2), down_parts(2)])
    ys = jnp.stack([y, (y + 3) % 4, (y + 1) % 4, (y + 2) % 4]).astype(jnp.int32)

    here, there = xh * 4, (1 - xh) * 4
    wslots = jnp.stack(
        [here + z, here + (z + 3) % 4, here + (z + 1) % 4, here + (z + 2) % 4]
        + [there + z, there + (z + 3) % 4, there + (z + 1) % 4, there + (z + 2) % 4]
    ).astype(jnp.int32)
    whigh, wlow = prep_w(wslots, [w, wp, wm, w2, wx, wxp, wxm, wx2])

    gap = vir_energy[:, None] - occ_energy[None, :]
    first = (xh * 4 + z) * virtuals
    row_gap = lax.dynamic_slice_in_dim(gap, first, virtuals)
    rgap = jnp.broadcast_to(row_gap.reshape(virtuals, 4, 8, 1), (virtuals, 4, 8, 128))
    start = ((y * 2 + xl) * 2 + core) * columns
    cgap = lax.dynamic_slice_in_dim(gap.reshape(-1), start, columns).reshape(1, columns)

    out = matmul(ys, parts, whigh.reshape(depth, columns), wlow.reshape(depth, columns), rgap, cgap, virtuals)
    return out.reshape(virtuals * 32, columns)


def solution(mesh):
    fine = Mesh(mesh.devices.reshape(SIZES), AXES)
    in_specs = (P(COL, ROW, None, None), P(COL, ROW), P(), P())
    return jax.shard_map(body, mesh=fine, in_specs=in_specs, out_specs=P(COL, ROW), check_vma=False)
```

```python
import functools

import jax
import jax.numpy as jnp
import numpy as np
from jax import lax
from jax.experimental import pallas as pl
from jax.experimental.pallas import tpu as pltpu
from jax.sharding import Mesh, PartitionSpec as P

ROW = ("y", "xl", "core")
COL = ("xh", "z")
AXES = ROW + COL
SIZES = (4, 2, 2, 2, 4)
f32, bf16 = jnp.float32, jnp.bfloat16
MIB = 1 << 20
HALF = 64


def hop(value, **move):
    pairs = []
    for source in range(int(np.prod(SIZES))):
        place = list(np.unravel_index(source, SIZES))
        for axis, step in move.items():
            k = AXES.index(axis)
            place[k] = (place[k] + step) % SIZES[k]
        pairs.append((source, int(np.ravel_multi_index(place, SIZES))))
    return lax.ppermute(value, AXES, pairs)


def after(value, *needed):
    return lax.optimization_barrier((value,) + needed)[0]


def split(value):
    high = value.astype(bf16)
    return high, (value - high.astype(f32)).astype(bf16)


def turn_kernel(amp_ref, out_ref):
    for n in range(out_ref.shape[0]):
        lanes = slice(n * 128, n * 128 + 128)
        both = jnp.concatenate([amp_ref[0, lanes], amp_ref[1, lanes]], axis=1)
        out_ref[n] = both.T


def turn(amp):
    two, depth, width = amp.shape
    return pl.pallas_call(
        turn_kernel,
        out_shape=jax.ShapeDtypeStruct((depth // 128, two * width, 128), f32),
        in_specs=[pl.BlockSpec(memory_space=pltpu.VMEM)],
        out_specs=pl.BlockSpec(memory_space=pltpu.VMEM),
        name="turn",
    )(amp)


def dense(info_ref, held, order, high_refs, low_refs):
    width = held.shape[1] // 8
    for h in range(2):
        base = info_ref[order + h] * 4
        for k in range(4):
            block = held.at[base + k]
            for a in range(0, width, 2):
                value = jnp.concatenate([block[pl.ds(a + b, 8, stride=width), :] for b in range(2)], axis=0)
                high, low = split(value)
                high_refs[h][a * 8 : a * 8 + 16, k * 128 : k * 128 + 128] = high
                low_refs[h][a * 8 : a * 8 + 16, k * 128 : k * 128 + 128] = low


def three(high, low, whigh, wlow):
    total = jnp.dot(high, whigh, preferred_element_type=f32)
    total += jnp.dot(high, wlow, preferred_element_type=f32)
    return total + jnp.dot(low, whigh, preferred_element_type=f32)


def pull(info_ref, held, sems, pieces):
    copies = []
    for n, (ref, start, rows, slot, offset) in enumerate(pieces):
        row = pl.multiple_of(info_ref[slot] * (2 * HALF) + offset, 8)
        copies.append(pltpu.make_async_copy(ref.at[:, pl.ds(start, rows)], held.at[:, pl.ds(row, rows)], sems.at[n]))
    return copies


def pull_w(info_ref, held, sems, refs):
    return [pltpu.make_async_copy(ref, held.at[info_ref[8 + n]], sems.at[n]) for n, ref in enumerate(refs)]


def early_kernel(info_ref, x, xx, s1, xp, xxp, xm, xxm, s2, w, wp, wm, w2,
                 part_ref, ahigh_ref, alow_ref, whigh_ref, wlow_ref, held, wheld, high, low, sems, wsems):
    chunk = pl.program_id(0)
    both = 2 * HALF
    sets = [
        [(x, 0, both, 0, 0), (xx, 0, both, 1, 0), (s1, 0, both, 2, 0), (s1, both, both, 3, 0)],
        [(xp, 0, both, 0, 0), (xxp, 0, both, 1, 0), (s1, 2 * both, both, 2, 0), (s2, 0, both, 3, 0)],
        [(xm, 0, both, 0, 0), (xxm, 0, both, 1, 0), (s1, 3 * both, both, 2, 0), (s2, both, both, 3, 0)],
    ]
    copies = [pull(info_ref, held.at[j], sems.at[j], sets[j]) for j in range(3)]
    wcopies = pull_w(info_ref, wheld, wsems, [w, wp, wm, w2])

    @pl.when(chunk == 0)
    def _():
        for copy in copies[0] + wcopies + copies[1] + copies[2]:
            copy.start()
        for copy in wcopies:
            copy.wait()
        for n in range(4):
            h, l = split(wheld[n])
            whigh_ref[n * 128 : n * 128 + 128] = h
            wlow_ref[n * 128 : n * 128 + 128] = l

    for j in range(3):
        @pl.when(chunk == j)
        def _():
            for copy in copies[j]:
                copy.wait()

    dense(info_ref, held.at[chunk], 12, [high, ahigh_ref], [low, alow_ref])
    for n in range(0, part_ref.shape[1], 256):
        part_ref[:, n : n + 256] = three(high[...], low[...], whigh_ref[:, n : n + 256], wlow_ref[:, n : n + 256])


def early(info, sources, weights):
    columns = weights[0].shape[1]
    rows = 8 * HALF
    depth = 4 * 128
    return pl.pallas_call(
        early_kernel,
        out_shape=[
            jax.ShapeDtypeStruct((3 * rows, columns), f32),
            jax.ShapeDtypeStruct((3 * rows, depth), bf16),
            jax.ShapeDtypeStruct((3 * rows, depth), bf16),
            jax.ShapeDtypeStruct((depth, columns), bf16),
            jax.ShapeDtypeStruct((depth, columns), bf16),
        ],
        grid_spec=pltpu.PrefetchScalarGridSpec(
            num_scalar_prefetch=1,
            grid=(3,),
            in_specs=[pl.BlockSpec(memory_space=pltpu.HBM)] * 12,
            out_specs=[
                pl.BlockSpec((rows, columns), lambda c, i: (c, 0)),
                pl.BlockSpec((rows, depth), lambda c, i: (c, 0)),
                pl.BlockSpec((rows, depth), lambda c, i: (c, 0)),
                pl.BlockSpec((depth, columns), lambda c, i: (0, 0)),
                pl.BlockSpec((depth, columns), lambda c, i: (0, 0)),
            ],
            scratch_shapes=[
                pltpu.VMEM((3, 8, rows, 128), f32),
                pltpu.VMEM((4, 128, columns), f32),
                pltpu.VMEM((rows, depth), bf16),
                pltpu.VMEM((rows, depth), bf16),
                pltpu.SemaphoreType.DMA((3, 4)),
                pltpu.SemaphoreType.DMA((4,)),
            ],
        ),
        compiler_params=pltpu.CompilerParams(vmem_limit_bytes=60 * MIB),
        cost_estimate=pl.CostEstimate(flops=18 * rows * depth * columns, bytes_accessed=20 * MIB, transcendentals=0),
        name="early",
    )(info, *sources, *weights)


def late_kernel(info_ref, part_ref, ahigh_ref, alow_ref, whigh_ref, wlow_ref, rgap_ref, cgap_ref,
                up, down, s3, wx, wxp, wxm, wx2,
                out_ref, held, wheld, whigh2, wlow2, high, low, high2, low2, sems, wsems):
    chunk = pl.program_id(0)
    last = 3
    columns = whigh_ref.shape[1]
    pieces = []
    for ref, base, slot in ((up, 0, 0), (down, 0, 0), (s3, 0, 2), (s3, 2 * HALF, 2)):
        offset = HALF * (len(pieces) // 2 % 2)
        pieces += [(ref, base, HALF, slot, offset), (ref, base + HALF, HALF, slot + 1, offset)]
    copies = pull(info_ref, held, sems, pieces)
    wcopies = pull_w(info_ref, wheld, wsems, [wx, wxp, wxm, wx2])

    @pl.when(chunk == 0)
    def _():
        for copy in wcopies + copies:
            copy.start()
        for copy in wcopies:
            copy.wait()
        for n in range(4):
            h, l = split(wheld[n])
            whigh2[n * 128 : n * 128 + 128] = h
            wlow2[n * 128 : n * 128 + 128] = l

    tall = rgap_ref[...].reshape(-1, 128)

    def finish(n, total):
        for m in range(0, 256, 128):
            gap = tall + cgap_ref[:, n + m : n + m + 128]
            out_ref[:, 0, :, n + m : n + m + 128] = (total[:, m : m + 128] / gap).reshape(-1, 8, 128)

    @pl.when(chunk < last)
    def _():
        for n in range(0, columns, 256):
            cut = slice(n, n + 256)
            total = part_ref[:, cut] + three(ahigh_ref[...], alow_ref[...], whigh2[:, cut], wlow2[:, cut])
            finish(n, total)

    @pl.when(chunk == last)
    def _():
        for copy in copies:
            copy.wait()
        dense(info_ref, held, 12, [high, high2], [low, low2])
        for n in range(0, columns, 256):
            cut = slice(n, n + 256)
            total = three(high[...], low[...], whigh_ref[:, cut], wlow_ref[:, cut])
            total += three(high2[...], low2[...], whigh2[:, cut], wlow2[:, cut])
            finish(n, total)


def late(info, made, rgap, cgap, sources, weights, virtuals):
    columns = weights[0].shape[1]
    rows = 8 * HALF
    depth = 4 * 128
    block = lambda width: pl.BlockSpec((rows, width), lambda c, i: (jnp.minimum(c, 2), 0))
    fixed = lambda *shape: pl.BlockSpec(shape, lambda c, i: (0, 0))
    return pl.pallas_call(
        late_kernel,
        out_shape=jax.ShapeDtypeStruct((virtuals, 4, 8, columns), f32),
        grid_spec=pltpu.PrefetchScalarGridSpec(
            num_scalar_prefetch=1,
            grid=(4,),
            in_specs=[block(columns), block(depth), block(depth), fixed(depth, columns), fixed(depth, columns)]
            + [pl.BlockSpec((virtuals, 1, 8, 128), lambda c, i: (0, i[4 + c], 0, 0)), fixed(1, columns)]
            + [pl.BlockSpec(memory_space=pltpu.HBM)] * 7,
            out_specs=pl.BlockSpec((virtuals, 1, 8, columns), lambda c, i: (0, i[4 + c], 0, 0)),
            scratch_shapes=[
                pltpu.VMEM((8, rows, 128), f32),
                pltpu.VMEM((4, 128, columns), f32),
                pltpu.VMEM((depth, columns), bf16),
                pltpu.VMEM((depth, columns), bf16),
            ]
            + [pltpu.VMEM((rows, depth), bf16)] * 4
            + [pltpu.SemaphoreType.DMA((8,)), pltpu.SemaphoreType.DMA((4,))],
        ),
        compiler_params=pltpu.CompilerParams(vmem_limit_bytes=60 * MIB),
        cost_estimate=pl.CostEstimate(flops=30 * rows * depth * columns, bytes_accessed=24 * MIB, transcendentals=0),
        name="late",
    )(info, *made, rgap, cgap, *sources, *weights)


def body(amplitudes, integrals, occ_energy, vir_energy):
    virtuals, own = amplitudes.shape[:2]
    depth = amplitudes.shape[2] * amplitudes.shape[3]
    columns = integrals.shape[1]
    y, xl, core, xh, z = (lax.axis_index(a) for a in AXES)

    info = jnp.stack(
        [xl * 2 + core, (1 - xl) * 2 + core, xl * 2 + 1 - core, (1 - xl) * 2 + 1 - core]
        + [y, (y + 3) % 4, (y + 1) % 4, (y + 2) % 4]
        + [z, (z + 3) % 4, (z + 1) % 4, (z + 2) % 4]
        + [xh, 1 - xh]
    ).astype(jnp.int32)
    gap = vir_energy[:, None] - occ_energy[None, :]
    row_gap = lax.dynamic_slice_in_dim(gap, (xh * 4 + z) * virtuals, virtuals)
    rgap = jnp.broadcast_to(row_gap.reshape(virtuals, 4, 8, 1), (virtuals, 4, 8, 128))
    start = ((y * 2 + xl) * 2 + core) * columns
    cgap = lax.dynamic_slice_in_dim(gap.reshape(-1), start, columns).reshape(1, columns)
    info, rgap, cgap = lax.optimization_barrier((info, rgap, cgap))

    join = lambda *values: jnp.concatenate(values, axis=1)
    x = turn(amplitudes.transpose(1, 2, 3, 0).reshape(own, depth, virtuals))
    w = integrals

    wp, wm = hop(w, z=1), hop(w, z=3)
    xp, xm, xx = hop(x, y=1), hop(x, y=3), hop(x, xl=1)
    wp, wm, xp, xm, xx, w, x = lax.optimization_barrier((wp, wm, xp, xm, xx, w, x))
    xxp, xxm, w2, wx = hop(xx, y=1), hop(xx, y=3), hop(w, z=2), hop(w, xh=1)
    s1 = hop(join(x, xx, xp, xm), core=1)
    xxp, xxm, w2, wx, s1 = lax.optimization_barrier((xxp, xxm, w2, wx, s1))
    s2 = hop(join(xxp, xxm), core=1)
    up = hop(join(xp[:, :HALF], xxp[:, :HALF]), y=1)
    down = hop(join(xm[:, HALF:], xxm[:, HALF:]), y=3)
    wxp, wxm, wx2 = hop(wx, z=1), hop(wx, z=3), hop(w2, xh=1)
    made = early(info, [x, xx, s1, xp, xxp, xm, xxm, s2], [w, wp, wm, w2])
    up, down, wxp, wxm, wx2, *made = lax.optimization_barrier((up, down, wxp, wxm, wx2, *made))
    s3 = hop(join(up, down), core=1)
    out = late(info, made, rgap, cgap, [up, down, s3], [wx, wxp, wxm, wx2], virtuals)
    return out.reshape(virtuals * 32, columns)


def solution(mesh):
    fine = Mesh(mesh.devices.reshape(SIZES), AXES)
    in_specs = (P(COL, ROW, None, None), P(COL, ROW), P(), P())
    return jax.shard_map(body, mesh=fine, in_specs=in_specs, out_specs=P(COL, ROW), check_vma=False)
```

```python
import functools

import jax
import jax.numpy as jnp
import numpy as np
from jax import lax
from jax.experimental import pallas as pl
from jax.experimental.pallas import tpu as pltpu
from jax.sharding import Mesh, PartitionSpec as P

ROW = ("y", "xl", "core")
COL = ("xh", "z")
AXES = ROW + COL
SIZES = (4, 2, 2, 2, 4)
f32, bf16 = jnp.float32, jnp.bfloat16
MIB = 1 << 20
HALF = 64


def hop(value, **move):
    pairs = []
    for source in range(int(np.prod(SIZES))):
        place = list(np.unravel_index(source, SIZES))
        for axis, step in move.items():
            k = AXES.index(axis)
            place[k] = (place[k] + step) % SIZES[k]
        pairs.append((source, int(np.ravel_multi_index(place, SIZES))))
    return lax.ppermute(value, AXES, pairs)


def after(value, *needed):
    return lax.optimization_barrier((value,) + needed)[0]


def split(value):
    high = value.astype(bf16)
    return high, (value - high.astype(f32)).astype(bf16)


def turn_kernel(amp_ref, out_ref):
    for n in range(out_ref.shape[0]):
        lanes = slice(n * 128, n * 128 + 128)
        both = jnp.concatenate([amp_ref[0, lanes], amp_ref[1, lanes]], axis=1)
        out_ref[n] = both.T


def turn(amp):
    two, depth, width = amp.shape
    return pl.pallas_call(
        turn_kernel,
        out_shape=jax.ShapeDtypeStruct((depth // 128, two * width, 128), f32),
        in_specs=[pl.BlockSpec(memory_space=pltpu.VMEM)],
        out_specs=pl.BlockSpec(memory_space=pltpu.VMEM),
        name="turn",
    )(amp)


def dense(info_ref, held, order, high_refs, low_refs):
    width = held.shape[1] // 8
    for h in range(2):
        base = info_ref[order + h] * 4
        for k in range(4):
            block = held.at[base + k]
            for a in range(0, width, 2):
                value = jnp.concatenate([block[pl.ds(a + b, 8, stride=width), :] for b in range(2)], axis=0)
                high, low = split(value)
                high_refs[h][a * 8 : a * 8 + 16, k * 128 : k * 128 + 128] = high
                low_refs[h][a * 8 : a * 8 + 16, k * 128 : k * 128 + 128] = low


def three(high, low, whigh, wlow):
    total = jnp.dot(high, whigh, preferred_element_type=f32)
    total += jnp.dot(high, wlow, preferred_element_type=f32)
    return total + jnp.dot(low, whigh, preferred_element_type=f32)


def pull(info_ref, held, sems, pieces):
    copies = []
    for n, (ref, start, rows, slot, offset) in enumerate(pieces):
        row = pl.multiple_of(info_ref[slot] * (2 * HALF) + offset, 8)
        copies.append(pltpu.make_async_copy(ref.at[:, pl.ds(start, rows)], held.at[:, pl.ds(row, rows)], sems.at[n]))
    return copies


def pull_w(info_ref, held, sems, refs):
    return [pltpu.make_async_copy(ref, held.at[info_ref[8 + n]], sems.at[n]) for n, ref in enumerate(refs)]


def early_kernel(info_ref, x, xx, s1, xp, xxp, xm, xxm, s2, w, wp, wm, w2,
                 part_ref, ahigh_ref, alow_ref, whigh_ref, wlow_ref, held, wheld, high, low, sems, wsems):
    chunk = pl.program_id(0)
    both = 2 * HALF
    sets = [
        [(x, 0, both, 0, 0), (xx, 0, both, 1, 0), (s1, 0, both, 2, 0), (s1, both, both, 3, 0)],
        [(xp, 0, both, 0, 0), (xxp, 0, both, 1, 0), (s1, 2 * both, both, 2, 0), (s2, 0, both, 3, 0)],
        [(xm, 0, both, 0, 0), (xxm, 0, both, 1, 0), (s1, 3 * both, both, 2, 0), (s2, both, both, 3, 0)],
    ]
    copies = [pull(info_ref, held.at[j], sems.at[j], sets[j]) for j in range(3)]
    wcopies = pull_w(info_ref, wheld, wsems, [w, wp, wm, w2])

    @pl.when(chunk == 0)
    def _():
        for copy in copies[0] + wcopies + copies[1] + copies[2]:
            copy.start()
        for copy in wcopies:
            copy.wait()
        for n in range(4):
            h, l = split(wheld[n])
            whigh_ref[n * 128 : n * 128 + 128] = h
            wlow_ref[n * 128 : n * 128 + 128] = l

    for j in range(3):
        @pl.when(chunk == j)
        def _():
            for copy in copies[j]:
                copy.wait()

    dense(info_ref, held.at[chunk], 12, [high, ahigh_ref.at[chunk]], [low, alow_ref.at[chunk]])
    for n in range(0, part_ref.shape[2], 256):
        part_ref[chunk, :, n : n + 256] = three(high[...], low[...], whigh_ref[:, n : n + 256], wlow_ref[:, n : n + 256])


def early(info, sources, weights):
    columns = weights[0].shape[1]
    rows = 8 * HALF
    depth = 4 * 128
    return pl.pallas_call(
        early_kernel,
        out_shape=[
            pltpu.VMEM((3, rows, columns), f32),
            pltpu.VMEM((3, rows, depth), bf16),
            pltpu.VMEM((3, rows, depth), bf16),
            pltpu.VMEM((depth, columns), bf16),
            pltpu.VMEM((depth, columns), bf16),
        ],
        grid_spec=pltpu.PrefetchScalarGridSpec(
            num_scalar_prefetch=1,
            grid=(3,),
            in_specs=[pl.BlockSpec(memory_space=pltpu.HBM)] * 12,
            out_specs=[pl.BlockSpec(memory_space=pltpu.VMEM)] * 5,
            scratch_shapes=[
                pltpu.VMEM((3, 8, rows, 128), f32),
                pltpu.VMEM((4, 128, columns), f32),
                pltpu.VMEM((rows, depth), bf16),
                pltpu.VMEM((rows, depth), bf16),
                pltpu.SemaphoreType.DMA((3, 4)),
                pltpu.SemaphoreType.DMA((4,)),
            ],
        ),
        compiler_params=pltpu.CompilerParams(vmem_limit_bytes=46 * MIB),
        cost_estimate=pl.CostEstimate(flops=18 * rows * depth * columns, bytes_accessed=20 * MIB, transcendentals=0),
        name="early",
    )(info, *sources, *weights)


def late_kernel(info_ref, part_ref, ahigh_ref, alow_ref, whigh_ref, wlow_ref, rgap_ref, cgap_ref,
                up, down, s3, wx, wxp, wxm, wx2,
                out_ref, held, wheld, whigh2, wlow2, high, low, high2, low2, sems, wsems):
    chunk = pl.program_id(0)
    last = 3
    columns = whigh_ref.shape[1]
    pieces = []
    for ref, base, slot in ((up, 0, 0), (down, 0, 0), (s3, 0, 2), (s3, 2 * HALF, 2)):
        offset = HALF * (len(pieces) // 2 % 2)
        pieces += [(ref, base, HALF, slot, offset), (ref, base + HALF, HALF, slot + 1, offset)]
    copies = pull(info_ref, held, sems, pieces)
    wcopies = pull_w(info_ref, wheld, wsems, [wx, wxp, wxm, wx2])

    @pl.when(chunk == 0)
    def _():
        for copy in wcopies + copies:
            copy.start()
        for copy in wcopies:
            copy.wait()
        for n in range(4):
            h, l = split(wheld[n])
            whigh2[n * 128 : n * 128 + 128] = h
            wlow2[n * 128 : n * 128 + 128] = l

    tall = rgap_ref[...].reshape(-1, 128)

    def finish(n, total):
        for m in range(0, 256, 128):
            gap = tall + cgap_ref[:, n + m : n + m + 128]
            out_ref[:, 0, :, n + m : n + m + 128] = (total[:, m : m + 128] / gap).reshape(-1, 8, 128)

    @pl.when(chunk < last)
    def _():
        for n in range(0, columns, 256):
            cut = slice(n, n + 256)
            total = part_ref[chunk, :, cut] + three(ahigh_ref[chunk], alow_ref[chunk], whigh2[:, cut], wlow2[:, cut])
            finish(n, total)

    @pl.when(chunk == last)
    def _():
        for copy in copies:
            copy.wait()
        dense(info_ref, held, 12, [high, high2], [low, low2])
        for n in range(0, columns, 256):
            cut = slice(n, n + 256)
            total = three(high[...], low[...], whigh_ref[:, cut], wlow_ref[:, cut])
            total += three(high2[...], low2[...], whigh2[:, cut], wlow2[:, cut])
            finish(n, total)


def late(info, made, rgap, cgap, sources, weights, virtuals):
    columns = weights[0].shape[1]
    rows = 8 * HALF
    depth = 4 * 128
    fixed = lambda *shape: pl.BlockSpec(shape, lambda c, i: (0, 0))
    return pl.pallas_call(
        late_kernel,
        out_shape=jax.ShapeDtypeStruct((virtuals, 4, 8, columns), f32),
        grid_spec=pltpu.PrefetchScalarGridSpec(
            num_scalar_prefetch=1,
            grid=(4,),
            in_specs=[pl.BlockSpec(memory_space=pltpu.VMEM)] * 5
            + [pl.BlockSpec((virtuals, 1, 8, 128), lambda c, i: (0, i[4 + c], 0, 0)), fixed(1, columns)]
            + [pl.BlockSpec(memory_space=pl.ANY)] * 7,
            out_specs=pl.BlockSpec((virtuals, 1, 8, columns), lambda c, i: (0, i[4 + c], 0, 0)),
            scratch_shapes=[
                pltpu.VMEM((8, rows, 128), f32),
                pltpu.VMEM((4, 128, columns), f32),
                pltpu.VMEM((depth, columns), bf16),
                pltpu.VMEM((depth, columns), bf16),
            ]
            + [pltpu.VMEM((rows, depth), bf16)] * 4
            + [pltpu.SemaphoreType.DMA((8,)), pltpu.SemaphoreType.DMA((4,))],
        ),
        compiler_params=pltpu.CompilerParams(vmem_limit_bytes=30 * MIB),
        cost_estimate=pl.CostEstimate(flops=30 * rows * depth * columns, bytes_accessed=24 * MIB, transcendentals=0),
        name="late",
    )(info, *(pltpu.with_memory_space_constraint(v, pltpu.VMEM) for v in made), rgap, cgap, *sources, *weights)


def body(amplitudes, integrals, occ_energy, vir_energy):
    virtuals, own = amplitudes.shape[:2]
    depth = amplitudes.shape[2] * amplitudes.shape[3]
    columns = integrals.shape[1]
    y, xl, core, xh, z = (lax.axis_index(a) for a in AXES)

    info = jnp.stack(
        [xl * 2 + core, (1 - xl) * 2 + core, xl * 2 + 1 - core, (1 - xl) * 2 + 1 - core]
        + [y, (y + 3) % 4, (y + 1) % 4, (y + 2) % 4]
        + [z, (z + 3) % 4, (z + 1) % 4, (z + 2) % 4]
        + [xh, 1 - xh]
    ).astype(jnp.int32)
    gap = vir_energy[:, None] - occ_energy[None, :]
    row_gap = lax.dynamic_slice_in_dim(gap, (xh * 4 + z) * virtuals, virtuals)
    rgap = jnp.broadcast_to(row_gap.reshape(virtuals, 4, 8, 1), (virtuals, 4, 8, 128))
    start = ((y * 2 + xl) * 2 + core) * columns
    cgap = lax.dynamic_slice_in_dim(gap.reshape(-1), start, columns).reshape(1, columns)

    join = lambda *values: jnp.concatenate(values, axis=1)
    x = turn(amplitudes.transpose(1, 2, 3, 0).reshape(own, depth, virtuals))
    w = integrals

    wp, wm = hop(w, z=1), hop(w, z=3)
    xp, xm, xx = hop(x, y=1), hop(x, y=3), hop(x, xl=1)
    xx, wp, wm, info, rgap, cgap = lax.optimization_barrier((xx, wp, wm, info, rgap, cgap))
    xxp, xxm = hop(xx, y=1), hop(xx, y=3)
    w2, wx = hop(after(w, wp, wm), z=2), hop(after(w, xx), xh=1)
    s1 = hop(join(x, xx, xp, xm), core=1)
    xxp, xxm, w2, wx, s1 = lax.optimization_barrier((xxp, xxm, w2, wx, s1))
    s2 = hop(join(xxp, xxm), core=1)
    up = hop(join(xp[:, :HALF], xxp[:, :HALF]), y=1)
    down = hop(join(xm[:, HALF:], xxm[:, HALF:]), y=3)
    wxp, wxm, wx2 = hop(wx, z=1), hop(wx, z=3), hop(w2, xh=1)

    *made, wlow = early(info, [x, xx, s1, xp, xxp, xm, xxm, s2], [w, wp, wm, w2])
    up, down, wxp, wxm, wx2, wlow = lax.optimization_barrier((up, down, wxp, wxm, wx2, wlow))
    s3 = hop(join(up, down), core=1)
    made += [wlow]
    out = late(info, made, rgap, cgap, [up, down, s3], [wx, wxp, wxm, wx2], virtuals)
    return out.reshape(virtuals * 32, columns)


def solution(mesh):
    fine = Mesh(mesh.devices.reshape(SIZES), AXES)
    in_specs = (P(COL, ROW, None, None), P(COL, ROW), P(), P())
    return jax.shard_map(body, mesh=fine, in_specs=in_specs, out_specs=P(COL, ROW), check_vma=False)
```

```python
import functools

import jax
import jax.numpy as jnp
import numpy as np
from jax import lax
from jax.experimental import pallas as pl
from jax.experimental.pallas import tpu as pltpu
from jax.sharding import Mesh, PartitionSpec as P

ROW = ("y", "xl", "core")
COL = ("xh", "z")
AXES = ROW + COL
SIZES = (4, 2, 2, 2, 4)
f32, bf16 = jnp.float32, jnp.bfloat16
MIB = 1 << 20
READY, EARLY, LATE, LAST = 40, 42, 24, 24
TURN_FLOPS = 1 << 20
HALF = 64


def hop(value, **move):
    pairs = []
    for source in range(int(np.prod(SIZES))):
        place = list(np.unravel_index(source, SIZES))
        for axis, step in move.items():
            k = AXES.index(axis)
            place[k] = (place[k] + step) % SIZES[k]
        pairs.append((source, int(np.ravel_multi_index(place, SIZES))))
    return lax.ppermute(value, AXES, pairs)


def after(value, *needed):
    return lax.optimization_barrier((value,) + needed)[0]


def split(value):
    high = value.astype(bf16)
    return high, (value - high.astype(f32)).astype(bf16)


def turn_kernel(amp_ref, out_ref):
    for n in range(out_ref.shape[0]):
        lanes = slice(n * 128, n * 128 + 128)
        both = jnp.concatenate([amp_ref[0, lanes], amp_ref[1, lanes]], axis=1)
        out_ref[n] = both.T


def turn(amp):
    two, depth, width = amp.shape
    return pl.pallas_call(
        turn_kernel,
        out_shape=jax.ShapeDtypeStruct((depth // 128, two * width, 128), f32),
        in_specs=[pl.BlockSpec(memory_space=pltpu.VMEM)],
        out_specs=pl.BlockSpec(memory_space=pltpu.VMEM),
        cost_estimate=pl.CostEstimate(flops=TURN_FLOPS, bytes_accessed=2 * MIB, transcendentals=0),
        name="turn",
    )(amp)


def dense(info_ref, held, high_refs, low_refs, rows=slice(0, 64)):
    width = held.shape[1] // 8
    for h in range(2):
        base = info_ref[12 + h] * 4
        for k in range(4):
            block = held.at[base + info_ref[8 + k]]
            for a in range(rows.start, rows.stop, 2):
                value = jnp.concatenate([block[pl.ds(a + b, 8, stride=width), :] for b in range(2)], axis=0)
                high, low = split(value)
                high_refs[h][a * 8 : a * 8 + 16, k * 128 : k * 128 + 128] = high
                low_refs[h][a * 8 : a * 8 + 16, k * 128 : k * 128 + 128] = low


def three(high, low, whigh, wlow):
    total = jnp.dot(high, whigh, preferred_element_type=f32)
    total += jnp.dot(high, wlow, preferred_element_type=f32)
    return total + jnp.dot(low, whigh, preferred_element_type=f32)


def pull(info_ref, held, sems, pieces):
    copies = []
    for n, (ref, start, rows, slot, offset) in enumerate(pieces):
        row = pl.multiple_of(info_ref[slot] * (2 * HALF) + offset, 8)
        copies.append(pltpu.make_async_copy(ref.at[:, pl.ds(start, rows)], held.at[:, pl.ds(row, rows)], sems.at[n]))
    return copies


def start_all(copies):
    for copy in copies:
        copy.start()


def wait_all(copies):
    for copy in copies:
        copy.wait()


def split_into(high_ref, low_ref, pieces, first=0):
    for n, ref in enumerate(pieces):
        row = (first + n) * 128
        high_ref[row : row + 128], low_ref[row : row + 128] = split(ref[...])


WHOLE = pl.BlockSpec(memory_space=pltpu.VMEM)
APART = pl.BlockSpec(memory_space=pltpu.HBM)
ANYWHERE = pl.BlockSpec(memory_space=pl.ANY)
ROWS = 8 * HALF
DEEP = 512
near = lambda value: pltpu.with_memory_space_constraint(value, pltpu.VMEM)


def ready_kernel(info_ref, x, xx, s1, w, wp, wm, high, low, high2, low2, whigh, wlow, held, sems):
    both = 2 * HALF
    copies = pull(info_ref, held, sems, [(x, 0, both, 0, 0), (xx, 0, both, 1, 0), (s1, 0, both, 2, 0), (s1, both, both, 3, 0)])
    start_all(copies)
    split_into(whigh, wlow, [w, wp, wm])
    wait_all(copies)
    dense(info_ref, held, [high, high2], [low, low2])


def ready(info, sources, weights):
    columns = weights[0].shape[1]
    return pl.pallas_call(
        ready_kernel,
        out_shape=[pltpu.VMEM((ROWS, DEEP), bf16)] * 4 + [pltpu.VMEM((384, columns), bf16)] * 2,
        in_specs=[pl.BlockSpec(memory_space=pltpu.SMEM)] + [APART] * 3 + [WHOLE] * 3,
        out_specs=[WHOLE] * 6,
        scratch_shapes=[pltpu.VMEM((8, ROWS, 128), f32), pltpu.SemaphoreType.DMA((4,))],
        compiler_params=pltpu.CompilerParams(vmem_limit_bytes=READY * MIB),
        cost_estimate=pl.CostEstimate(flops=4 * ROWS * DEEP, bytes_accessed=10 * MIB, transcendentals=0),
        name="ready",
    )(info, *sources, *weights)


def early_kernel(info_ref, s2, xp, xxp, xm, xxm, w2, high, low, whigh3, wlow3,
                 part_ref, ahigh_ref, alow_ref, whigh, wlow, held, bhigh, blow, sems):
    both = 2 * HALF
    copies = [
        pull(info_ref, held.at[j], sems.at[j], [
            (near_ref, 0, both, 0, 0), (far_ref, 0, both, 1, 0), (s2, 2 * j * both, both, 2, 0), (s2, (2 * j + 1) * both, both, 3, 0)
        ])
        for j, (near_ref, far_ref) in enumerate(((xp, xxp), (xm, xxm)))
    ]
    start_all(copies[0] + copies[1])
    whigh[0:384] = whigh3[...]
    wlow[0:384] = wlow3[...]
    split_into(whigh, wlow, [w2], 3)
    for j in range(3):
        if j:
            wait_all(copies[j - 1])
            dense(info_ref, held.at[j - 1], [bhigh.at[j - 1], ahigh_ref.at[j - 1]], [blow.at[j - 1], alow_ref.at[j - 1]])
        h, l = (high, low) if j == 0 else (bhigh.at[j - 1], blow.at[j - 1])
        for n in range(0, part_ref.shape[2], 256):
            part_ref[j, :, n : n + 256] = three(h[...], l[...], whigh[:, n : n + 256], wlow[:, n : n + 256])


def early(info, sources, w2, made):
    columns = w2.shape[1]
    return pl.pallas_call(
        early_kernel,
        out_shape=[
            pltpu.VMEM((3, ROWS, columns), f32),
            pltpu.VMEM((2, ROWS, DEEP), bf16),
            pltpu.VMEM((2, ROWS, DEEP), bf16),
            pltpu.VMEM((DEEP, columns), bf16),
            pltpu.VMEM((DEEP, columns), bf16),
        ],
        in_specs=[pl.BlockSpec(memory_space=pltpu.SMEM)] + [APART] * 5 + [WHOLE] * 5,
        out_specs=[WHOLE] * 5,
        scratch_shapes=[
            pltpu.VMEM((2, 8, ROWS, 128), f32),
            pltpu.VMEM((2, ROWS, DEEP), bf16),
            pltpu.VMEM((2, ROWS, DEEP), bf16),
            pltpu.SemaphoreType.DMA((2, 4)),
        ],
        compiler_params=pltpu.CompilerParams(vmem_limit_bytes=EARLY * MIB),
        cost_estimate=pl.CostEstimate(flops=18 * ROWS * DEEP * columns, bytes_accessed=20 * MIB, transcendentals=0),
        name="early",
    )(info, *sources, w2, *(near(v) for v in made))


def finish(out_ref, rgap_ref, cgap_ref, n, total):
    tall = rgap_ref[...].reshape(-1, 128)
    for m in range(0, 256, 128):
        gap = tall + cgap_ref[:, n + m : n + m + 128]
        out_ref[:, 0, :, n + m : n + m + 128] = (total[:, m : m + 128] / gap).reshape(-1, 8, 128)


def late_kernel(info_ref, part_ref, high2, low2, ahigh_ref, alow_ref, wx, wxp, wxm, wx2, rgap_ref, cgap_ref,
                out_ref, whigh2, wlow2):
    chunk = pl.program_id(0)

    @pl.when(chunk == 0)
    def _():
        split_into(whigh2, wlow2, [wx, wxp, wxm, wx2])

    def work(h, l):
        for n in range(0, whigh2.shape[1], 256):
            cut = slice(n, n + 256)
            finish(out_ref, rgap_ref, cgap_ref, n, part_ref[chunk, :, cut] + three(h[...], l[...], whigh2[:, cut], wlow2[:, cut]))

    pl.when(chunk == 0)(lambda: work(high2, low2))
    pl.when(chunk > 0)(lambda: work(ahigh_ref.at[chunk - 1], alow_ref.at[chunk - 1]))


def late(info, part, own, others, weights, rgap, cgap, virtuals):
    columns = weights[0].shape[1]
    rows = lambda *shape: pl.BlockSpec((virtuals, 1, 8) + shape, lambda c, i: (0, i[4 + c], 0, 0))
    return pl.pallas_call(
        late_kernel,
        out_shape=[jax.ShapeDtypeStruct((virtuals, 4, 8, columns), f32)] + [pltpu.VMEM((DEEP, columns), bf16)] * 2,
        grid_spec=pltpu.PrefetchScalarGridSpec(
            num_scalar_prefetch=1,
            grid=(3,),
            in_specs=[WHOLE] * 9 + [rows(128), WHOLE],
            out_specs=[rows(columns), WHOLE, WHOLE],
        ),
        compiler_params=pltpu.CompilerParams(vmem_limit_bytes=LATE * MIB),
        cost_estimate=pl.CostEstimate(flops=18 * ROWS * DEEP * columns, bytes_accessed=24 * MIB, transcendentals=0),
        name="late",
    )(info, *(near(v) for v in (part, *own, *others)), *weights, rgap, cgap)


def last_kernel(info_ref, rest_ref, up, down, s3, whigh, wlow, whigh2, wlow2, rgap_ref, cgap_ref,
                out_ref, held, high, low, high2, low2, sems):
    del rest_ref
    step = pl.program_id(0)
    pieces = []
    for ref, base, slot in ((up, 0, 0), (down, 0, 0), (s3, 0, 2), (s3, 2 * HALF, 2)):
        offset = HALF * (len(pieces) // 2 % 2)
        pieces += [(ref, base, HALF, slot, offset), (ref, base + HALF, HALF, slot + 1, offset)]
    copies = pull(info_ref, held, sems, pieces)

    @pl.when(step == 0)
    def _():
        start_all(copies)
        wait_all(copies)
        dense(info_ref, held, [high, high2], [low, low2])

    part = pl.ds(pl.multiple_of(step * out_ref.shape[0] * 8, 16), out_ref.shape[0] * 8)
    for n in range(0, whigh.shape[1], 256):
        cut = slice(n, n + 256)
        total = three(high[part], low[part], whigh[:, cut], wlow[:, cut])
        total += three(high2[part], low2[part], whigh2[:, cut], wlow2[:, cut])
        finish(out_ref, rgap_ref, cgap_ref, n, total)


def last(info, rest, sources, weights, rgap, cgap, virtuals):
    columns = weights[0].shape[1]
    steps = 2
    rows = lambda *shape: pl.BlockSpec((virtuals // steps, 1, 8) + shape, lambda c, i: (c, i[7], 0, 0))
    return pl.pallas_call(
        last_kernel,
        out_shape=jax.ShapeDtypeStruct((virtuals, 4, 8, columns), f32),
        grid_spec=pltpu.PrefetchScalarGridSpec(
            num_scalar_prefetch=1,
            grid=(steps,),
            in_specs=[APART] + [ANYWHERE] * 3 + [WHOLE] * 4 + [rows(128), WHOLE],
            out_specs=rows(columns),
            scratch_shapes=[pltpu.VMEM((8, ROWS, 128), f32)]
            + [pltpu.VMEM((ROWS, DEEP), bf16)] * 4
            + [pltpu.SemaphoreType.DMA((8,))],
        ),
        input_output_aliases={1: 0},
        compiler_params=pltpu.CompilerParams(vmem_limit_bytes=LAST * MIB),
        cost_estimate=pl.CostEstimate(flops=12 * ROWS * DEEP * columns, bytes_accessed=8 * MIB, transcendentals=0),
        name="last",
    )(info, rest, *sources, *(near(v) for v in weights), rgap, cgap)


def body(amplitudes, integrals, occ_energy, vir_energy):
    virtuals, own = amplitudes.shape[:2]
    depth = amplitudes.shape[2] * amplitudes.shape[3]
    columns = integrals.shape[1]
    y, xl, core, xh, z = (lax.axis_index(a) for a in AXES)

    info = jnp.stack(
        [xl * 2 + core, (1 - xl) * 2 + core, xl * 2 + 1 - core, (1 - xl) * 2 + 1 - core]
        + [y, (y + 3) % 4, (y + 1) % 4, (y + 2) % 4]
        + [z, (z + 3) % 4, (z + 1) % 4, (z + 2) % 4]
        + [xh, 1 - xh]
    ).astype(jnp.int32)
    gap = vir_energy[:, None] - occ_energy[None, :]
    row_gap = lax.dynamic_slice_in_dim(gap, (xh * 4 + z) * virtuals, virtuals)
    rgap = jnp.broadcast_to(row_gap.reshape(virtuals, 4, 8, 1), (virtuals, 4, 8, 128))
    start = ((y * 2 + xl) * 2 + core) * columns
    cgap = lax.dynamic_slice_in_dim(gap.reshape(-1), start, columns).reshape(1, columns)

    join = lambda *values: jnp.concatenate(values, axis=1)
    x = turn(amplitudes.transpose(1, 2, 3, 0).reshape(own, depth, virtuals))
    w = integrals

    wp, wm = hop(w, z=1), hop(w, z=3)
    xp, xm, xx = hop(x, y=1), hop(x, y=3), hop(x, xl=1)
    xx, wp, wm, info, rgap, cgap = lax.optimization_barrier((xx, wp, wm, info, rgap, cgap))
    xxp, xxm = hop(xx, y=1), hop(xx, y=3)
    w2, wx = hop(after(w, wp, wm), z=2), hop(after(w, xx), xh=1)
    s1 = hop(after(join(x, xx), xp, xm), core=1)
    high, low, high2, low2, whigh, wlow = ready(info, [x, xx, s1], [w, wp, wm])
    xxp, xxm, w2, wx, wlow = lax.optimization_barrier((xxp, xxm, w2, wx, wlow))
    s2 = hop(join(xp, xxp, xm, xxm), core=1)
    up = hop(join(xp[:, :HALF], xxp[:, :HALF]), y=1)
    down = hop(join(xm[:, HALF:], xxm[:, HALF:]), y=3)
    wxp, wxm, wx2 = hop(wx, z=1), hop(wx, z=3), hop(w2, xh=1)

    part, ahigh, alow, whigh, wlow = early(info, [s2, xp, xxp, xm, xxm], w2, [high, low, whigh, wlow])
    up, down, wxp, wxm, wx2, wlow = lax.optimization_barrier((up, down, wxp, wxm, wx2, wlow))
    s3 = hop(join(up, down), core=1)
    out, whigh2, wlow2 = late(info, part, [high2, low2], [ahigh, alow], [wx, wxp, wxm, wx2], rgap, cgap, virtuals)
    out = last(info, out, [up, down, s3], [whigh, wlow, whigh2, wlow2], rgap, cgap, virtuals)
    return out.reshape(virtuals * 32, columns)


def solution(mesh):
    fine = Mesh(mesh.devices.reshape(SIZES), AXES)
    in_specs = (P(COL, ROW, None, None), P(COL, ROW), P(), P())
    return jax.shard_map(body, mesh=fine, in_specs=in_specs, out_specs=P(COL, ROW), check_vma=False)
```

```python
import functools

import jax
import jax.numpy as jnp
import numpy as np
from jax import lax
from jax.experimental import pallas as pl
from jax.experimental.pallas import tpu as pltpu
from jax.sharding import Mesh, PartitionSpec as P

ROW = ("y", "xl", "core")
COL = ("xh", "z")
AXES = ROW + COL
SIZES = (4, 2, 2, 2, 4)
f32, bf16 = jnp.float32, jnp.bfloat16
MIB = 1 << 20
READY, EARLY, LATE, LAST = 20, 24, 24, 24
TURN_FLOPS = 1 << 20
HALF = 64


def hop(value, **move):
    pairs = []
    for source in range(int(np.prod(SIZES))):
        place = list(np.unravel_index(source, SIZES))
        for axis, step in move.items():
            k = AXES.index(axis)
            place[k] = (place[k] + step) % SIZES[k]
        pairs.append((source, int(np.ravel_multi_index(place, SIZES))))
    return lax.ppermute(value, AXES, pairs)


def after(value, *needed):
    return lax.optimization_barrier((value,) + needed)[0]


def split(value):
    high = value.astype(bf16)
    return high, (value - high.astype(f32)).astype(bf16)


def turn_kernel(amp_ref, out_ref):
    for n in range(out_ref.shape[0]):
        lanes = slice(n * 128, n * 128 + 128)
        both = jnp.concatenate([amp_ref[0, lanes], amp_ref[1, lanes]], axis=1)
        out_ref[n] = both.T


def turn(amp):
    two, depth, width = amp.shape
    return pl.pallas_call(
        turn_kernel,
        out_shape=jax.ShapeDtypeStruct((depth // 128, two * width, 128), f32),
        in_specs=[pl.BlockSpec(memory_space=pltpu.VMEM)],
        out_specs=pl.BlockSpec(memory_space=pltpu.VMEM),
        cost_estimate=pl.CostEstimate(flops=TURN_FLOPS, bytes_accessed=2 * MIB, transcendentals=0),
        name="turn",
    )(amp)


def dense(info_ref, held, high_refs, low_refs, rows=slice(0, 64)):
    width = held.shape[1] // 8
    for h in range(2):
        base = info_ref[12 + h] * 4
        for k in range(4):
            block = held.at[base + info_ref[8 + k]]
            for a in range(rows.start, rows.stop, 2):
                value = jnp.concatenate([block[pl.ds(a + b, 8, stride=width), :] for b in range(2)], axis=0)
                high, low = split(value)
                high_refs[h][a * 8 : a * 8 + 16, k * 128 : k * 128 + 128] = high
                low_refs[h][a * 8 : a * 8 + 16, k * 128 : k * 128 + 128] = low


def three(high, low, whigh, wlow):
    total = jnp.dot(high, whigh, preferred_element_type=f32)
    total += jnp.dot(high, wlow, preferred_element_type=f32)
    return total + jnp.dot(low, whigh, preferred_element_type=f32)


def pull(info_ref, held, sems, pieces):
    copies = []
    for n, (ref, start, rows, slot, offset) in enumerate(pieces):
        row = pl.multiple_of(info_ref[slot] * (2 * HALF) + offset, 8)
        copies.append(pltpu.make_async_copy(ref.at[:, pl.ds(start, rows)], held.at[:, pl.ds(row, rows)], sems.at[n]))
    return copies


def start_all(copies):
    for copy in copies:
        copy.start()


def wait_all(copies):
    for copy in copies:
        copy.wait()


def split_into(high_ref, low_ref, pieces, first=0):
    for n, ref in enumerate(pieces):
        row = (first + n) * 128
        high_ref[row : row + 128], low_ref[row : row + 128] = split(ref[...])


WHOLE = pl.BlockSpec(memory_space=pltpu.VMEM)
APART = pl.BlockSpec(memory_space=pltpu.HBM)
ANYWHERE = pl.BlockSpec(memory_space=pl.ANY)
ROWS = 8 * HALF
DEEP = 512
near = lambda value: pltpu.with_memory_space_constraint(value, pltpu.VMEM)


def ready_kernel(info_ref, x, xx, s1, w, wp, wm, high, low, high2, low2, whigh, wlow, held, sems):
    both = 2 * HALF
    copies = pull(info_ref, held, sems, [(x, 0, both, 0, 0), (xx, 0, both, 1, 0), (s1, 0, both, 2, 0), (s1, both, both, 3, 0)])
    start_all(copies)
    split_into(whigh, wlow, [w, wp, wm])
    wait_all(copies)
    dense(info_ref, held, [high, high2], [low, low2])


def ready(info, sources, weights):
    columns = weights[0].shape[1]
    return pl.pallas_call(
        ready_kernel,
        out_shape=[pltpu.VMEM((ROWS, DEEP), bf16)] * 4 + [pltpu.VMEM((384, columns), bf16)] * 2,
        in_specs=[pl.BlockSpec(memory_space=pltpu.SMEM)] + [ANYWHERE] * 3 + [WHOLE] * 3,
        out_specs=[WHOLE] * 6,
        scratch_shapes=[pltpu.VMEM((8, ROWS, 128), f32), pltpu.SemaphoreType.DMA((4,))],
        compiler_params=pltpu.CompilerParams(vmem_limit_bytes=READY * MIB),
        cost_estimate=pl.CostEstimate(flops=4 * ROWS * DEEP, bytes_accessed=10 * MIB, transcendentals=0),
        name="ready",
    )(info, *sources, *weights)


def early_kernel(info_ref, s2, xp, xxp, xm, xxm, w2, high, low, whigh3, wlow3,
                 part_ref, ahigh_ref, alow_ref, whigh, wlow, held, bhigh, blow, sems):
    both = 2 * HALF
    copies = [
        pull(info_ref, held.at[j], sems.at[j], [
            (near_ref, 0, both, 0, 0), (far_ref, 0, both, 1, 0), (s2, 2 * j * both, both, 2, 0), (s2, (2 * j + 1) * both, both, 3, 0)
        ])
        for j, (near_ref, far_ref) in enumerate(((xp, xxp), (xm, xxm)))
    ]
    start_all(copies[0] + copies[1])
    whigh[0:384] = whigh3[...]
    wlow[0:384] = wlow3[...]
    split_into(whigh, wlow, [w2], 3)
    for j in range(3):
        if j:
            wait_all(copies[j - 1])
            dense(info_ref, held.at[j - 1], [bhigh.at[j - 1], ahigh_ref.at[j - 1]], [blow.at[j - 1], alow_ref.at[j - 1]])
        h, l = (high, low) if j == 0 else (bhigh.at[j - 1], blow.at[j - 1])
        for n in range(0, part_ref.shape[2], 256):
            part_ref[j, :, n : n + 256] = three(h[...], l[...], whigh[:, n : n + 256], wlow[:, n : n + 256])


def early(info, sources, w2, made):
    columns = w2.shape[1]
    return pl.pallas_call(
        early_kernel,
        out_shape=[
            pltpu.VMEM((3, ROWS, columns), f32),
            pltpu.VMEM((2, ROWS, DEEP), bf16),
            pltpu.VMEM((2, ROWS, DEEP), bf16),
            pltpu.VMEM((DEEP, columns), bf16),
            pltpu.VMEM((DEEP, columns), bf16),
        ],
        in_specs=[pl.BlockSpec(memory_space=pltpu.SMEM)] + [ANYWHERE] * 5 + [WHOLE] * 5,
        out_specs=[WHOLE] * 5,
        scratch_shapes=[
            pltpu.VMEM((2, 8, ROWS, 128), f32),
            pltpu.VMEM((2, ROWS, DEEP), bf16),
            pltpu.VMEM((2, ROWS, DEEP), bf16),
            pltpu.SemaphoreType.DMA((2, 4)),
        ],
        compiler_params=pltpu.CompilerParams(vmem_limit_bytes=EARLY * MIB),
        cost_estimate=pl.CostEstimate(flops=18 * ROWS * DEEP * columns, bytes_accessed=20 * MIB, transcendentals=0),
        name="early",
    )(info, *sources, w2, *(near(v) for v in made))


def finish(out_ref, rgap_ref, cgap_ref, n, total):
    tall = rgap_ref[...].reshape(-1, 128)
    for m in range(0, 256, 128):
        gap = tall + cgap_ref[:, n + m : n + m + 128]
        out_ref[:, 0, :, n + m : n + m + 128] = (total[:, m : m + 128] / gap).reshape(-1, 8, 128)


def late_kernel(info_ref, part_ref, high2, low2, ahigh_ref, alow_ref, wx, wxp, wxm, wx2, rgap_ref, cgap_ref,
                out_ref, whigh2, wlow2):
    chunk = pl.program_id(0)

    @pl.when(chunk == 0)
    def _():
        split_into(whigh2, wlow2, [wx, wxp, wxm, wx2])

    def work(h, l):
        for n in range(0, whigh2.shape[1], 256):
            cut = slice(n, n + 256)
            finish(out_ref, rgap_ref, cgap_ref, n, part_ref[chunk, :, cut] + three(h[...], l[...], whigh2[:, cut], wlow2[:, cut]))

    pl.when(chunk == 0)(lambda: work(high2, low2))
    pl.when(chunk > 0)(lambda: work(ahigh_ref.at[chunk - 1], alow_ref.at[chunk - 1]))


def late(info, part, own, others, weights, rgap, cgap, virtuals):
    columns = weights[0].shape[1]
    rows = lambda *shape: pl.BlockSpec((virtuals, 1, 8) + shape, lambda c, i: (0, i[4 + c], 0, 0))
    return pl.pallas_call(
        late_kernel,
        out_shape=[jax.ShapeDtypeStruct((virtuals, 4, 8, columns), f32)] + [pltpu.VMEM((DEEP, columns), bf16)] * 2,
        grid_spec=pltpu.PrefetchScalarGridSpec(
            num_scalar_prefetch=1,
            grid=(3,),
            in_specs=[WHOLE] * 9 + [rows(128), WHOLE],
            out_specs=[rows(columns), WHOLE, WHOLE],
        ),
        compiler_params=pltpu.CompilerParams(vmem_limit_bytes=LATE * MIB),
        cost_estimate=pl.CostEstimate(flops=18 * ROWS * DEEP * columns, bytes_accessed=24 * MIB, transcendentals=0),
        name="late",
    )(info, *(near(v) for v in (part, *own, *others)), *weights, rgap, cgap)


def last_kernel(info_ref, rest_ref, up, down, s3, whigh, wlow, whigh2, wlow2, rgap_ref, cgap_ref,
                out_ref, held, high, low, high2, low2, sems):
    del rest_ref
    step = pl.program_id(0)
    pieces = []
    for ref, base, slot in ((up, 0, 0), (down, 0, 0), (s3, 0, 2), (s3, 2 * HALF, 2)):
        offset = HALF * (len(pieces) // 2 % 2)
        pieces += [(ref, base, HALF, slot, offset), (ref, base + HALF, HALF, slot + 1, offset)]
    copies = pull(info_ref, held, sems, pieces)

    @pl.when(step == 0)
    def _():
        start_all(copies)
        wait_all(copies)
        dense(info_ref, held, [high, high2], [low, low2])

    part = pl.ds(pl.multiple_of(step * out_ref.shape[0] * 8, 16), out_ref.shape[0] * 8)
    for n in range(0, whigh.shape[1], 256):
        cut = slice(n, n + 256)
        total = three(high[part], low[part], whigh[:, cut], wlow[:, cut])
        total += three(high2[part], low2[part], whigh2[:, cut], wlow2[:, cut])
        finish(out_ref, rgap_ref, cgap_ref, n, total)


def last(info, rest, sources, weights, rgap, cgap, virtuals):
    columns = weights[0].shape[1]
    steps = 2
    rows = lambda *shape: pl.BlockSpec((virtuals // steps, 1, 8) + shape, lambda c, i: (c, i[7], 0, 0))
    return pl.pallas_call(
        last_kernel,
        out_shape=jax.ShapeDtypeStruct((virtuals, 4, 8, columns), f32),
        grid_spec=pltpu.PrefetchScalarGridSpec(
            num_scalar_prefetch=1,
            grid=(steps,),
            in_specs=[APART] + [ANYWHERE] * 3 + [WHOLE] * 4 + [rows(128), WHOLE],
            out_specs=rows(columns),
            scratch_shapes=[pltpu.VMEM((8, ROWS, 128), f32)]
            + [pltpu.VMEM((ROWS, DEEP), bf16)] * 4
            + [pltpu.SemaphoreType.DMA((8,))],
        ),
        input_output_aliases={1: 0},
        compiler_params=pltpu.CompilerParams(vmem_limit_bytes=LAST * MIB),
        cost_estimate=pl.CostEstimate(flops=12 * ROWS * DEEP * columns, bytes_accessed=8 * MIB, transcendentals=0),
        name="last",
    )(info, rest, *sources, *(near(v) for v in weights), rgap, cgap)


def body(amplitudes, integrals, occ_energy, vir_energy):
    virtuals, own = amplitudes.shape[:2]
    depth = amplitudes.shape[2] * amplitudes.shape[3]
    columns = integrals.shape[1]
    y, xl, core, xh, z = (lax.axis_index(a) for a in AXES)

    info = jnp.stack(
        [xl * 2 + core, (1 - xl) * 2 + core, xl * 2 + 1 - core, (1 - xl) * 2 + 1 - core]
        + [y, (y + 3) % 4, (y + 1) % 4, (y + 2) % 4]
        + [z, (z + 3) % 4, (z + 1) % 4, (z + 2) % 4]
        + [xh, 1 - xh]
    ).astype(jnp.int32)
    gap = vir_energy[:, None] - occ_energy[None, :]
    row_gap = lax.dynamic_slice_in_dim(gap, (xh * 4 + z) * virtuals, virtuals)
    rgap = jnp.broadcast_to(row_gap.reshape(virtuals, 4, 8, 1), (virtuals, 4, 8, 128))
    start = ((y * 2 + xl) * 2 + core) * columns
    cgap = lax.dynamic_slice_in_dim(gap.reshape(-1), start, columns).reshape(1, columns)

    join = lambda *values: jnp.concatenate(values, axis=1)
    x = turn(amplitudes.transpose(1, 2, 3, 0).reshape(own, depth, virtuals))
    w = integrals

    wp, wm = hop(w, z=1), hop(w, z=3)
    xp, xm, xx = hop(x, y=1), hop(x, y=3), hop(x, xl=1)
    xx, wp, wm, info, rgap, cgap = lax.optimization_barrier((xx, wp, wm, info, rgap, cgap))
    xxp, xxm = hop(xx, y=1), hop(xx, y=3)
    w2, wx = hop(after(w, wp, wm, xp), z=2), hop(after(w, xx, xm), xh=1)
    s1 = hop(join(x, xx), core=1)
    high, low, high2, low2, whigh, wlow = ready(info, [x, xx, s1], [w, wp, wm])
    xxp, xxm = lax.optimization_barrier((xxp, xxm))
    wx, w2, xxp, xxm, wlow = lax.optimization_barrier((wx, w2, xxp, xxm, wlow))
    s2 = hop(join(xp, xxp, xm, xxm), core=1)
    up = hop(join(xp[:, :HALF], xxp[:, :HALF]), y=1)
    down = hop(join(xm[:, HALF:], xxm[:, HALF:]), y=3)
    wxp, wxm, wx2 = hop(wx, z=1), hop(wx, z=3), hop(w2, xh=1)

    part, ahigh, alow, whigh, wlow = early(info, [s2, xp, xxp, xm, xxm], w2, [high, low, whigh, wlow])
    up, down, wxp, wxm, wx2, wlow = lax.optimization_barrier((up, down, wxp, wxm, wx2, wlow))
    s3 = hop(join(up, down), core=1)
    out, whigh2, wlow2 = late(info, part, [high2, low2], [ahigh, alow], [wx, wxp, wxm, wx2], rgap, cgap, virtuals)
    out = last(info, out, [up, down, s3], [whigh, wlow, whigh2, wlow2], rgap, cgap, virtuals)
    return out.reshape(virtuals * 32, columns)


def solution(mesh):
    fine = Mesh(mesh.devices.reshape(SIZES), AXES)
    in_specs = (P(COL, ROW, None, None), P(COL, ROW), P(), P())
    return jax.shard_map(body, mesh=fine, in_specs=in_specs, out_specs=P(COL, ROW), check_vma=False)
```

```python
import functools

import jax
import jax.numpy as jnp
import numpy as np
from jax import lax
from jax.experimental import pallas as pl
from jax.experimental.pallas import tpu as pltpu
from jax.sharding import Mesh, PartitionSpec as P

ROW = ("y", "xl", "core")
COL = ("xh", "z")
AXES = ROW + COL
SIZES = (4, 2, 2, 2, 4)
f32, bf16 = jnp.float32, jnp.bfloat16
MIB = 1 << 20
READY, EARLY, LATE, LAST = 20, 24, 24, 24
TURN_FLOPS = 1 << 20
HALF = 64


def hop(value, **move):
    pairs = []
    for source in range(int(np.prod(SIZES))):
        place = list(np.unravel_index(source, SIZES))
        for axis, step in move.items():
            k = AXES.index(axis)
            place[k] = (place[k] + step) % SIZES[k]
        pairs.append((source, int(np.ravel_multi_index(place, SIZES))))
    return lax.ppermute(value, AXES, pairs)


def after(value, *needed):
    return lax.optimization_barrier((value,) + needed)[0]


def split(value):
    high = value.astype(bf16)
    return high, (value - high.astype(f32)).astype(bf16)


def turn_kernel(amp_ref, out_ref):
    for n in range(out_ref.shape[0]):
        lanes = slice(n * 128, n * 128 + 128)
        both = jnp.concatenate([amp_ref[0, lanes], amp_ref[1, lanes]], axis=1)
        out_ref[n] = both.T


def turn(amp):
    two, depth, width = amp.shape
    return pl.pallas_call(
        turn_kernel,
        out_shape=jax.ShapeDtypeStruct((depth // 128, two * width, 128), f32),
        in_specs=[pl.BlockSpec(memory_space=pltpu.VMEM)],
        out_specs=pl.BlockSpec(memory_space=pltpu.VMEM),
        cost_estimate=pl.CostEstimate(flops=TURN_FLOPS, bytes_accessed=2 * MIB, transcendentals=0),
        name="turn",
    )(amp)


def dense(info_ref, held, high_refs, low_refs, rows=range(64)):
    width = held.shape[1] // 8
    for h in range(2):
        base = info_ref[12 + h] * 4
        for k in range(4):
            block = held.at[base + info_ref[8 + k]]
            for a in range(rows.start, rows.stop, 2):
                value = jnp.concatenate([block[pl.ds(a + b, 8, stride=width), :] for b in range(2)], axis=0)
                high, low = split(value)
                row = (a - rows.start) * 8
                high_refs[h][row : row + 16, k * 128 : k * 128 + 128] = high
                low_refs[h][row : row + 16, k * 128 : k * 128 + 128] = low


def three(high, low, whigh, wlow):
    total = jnp.dot(high, whigh, preferred_element_type=f32)
    total += jnp.dot(high, wlow, preferred_element_type=f32)
    return total + jnp.dot(low, whigh, preferred_element_type=f32)


def pull(info_ref, held, sems, pieces):
    copies = []
    for n, (ref, start, rows, slot, offset) in enumerate(pieces):
        row = pl.multiple_of(info_ref[slot] * (2 * HALF) + offset, 8)
        copies.append(pltpu.make_async_copy(ref.at[:, pl.ds(start, rows)], held.at[:, pl.ds(row, rows)], sems.at[n]))
    return copies


def start_all(copies):
    for copy in copies:
        copy.start()


def wait_all(copies):
    for copy in copies:
        copy.wait()


def split_into(high_ref, low_ref, pieces, first=0):
    for n, ref in enumerate(pieces):
        row = (first + n) * 128
        high_ref[row : row + 128], low_ref[row : row + 128] = split(ref[...])


WHOLE = pl.BlockSpec(memory_space=pltpu.VMEM)
APART = pl.BlockSpec(memory_space=pltpu.HBM)
ANYWHERE = pl.BlockSpec(memory_space=pl.ANY)
ROWS = 8 * HALF
DEEP = 512
near = lambda value: pltpu.with_memory_space_constraint(value, pltpu.VMEM)


def ready_kernel(info_ref, x, xx, s1, w, wp, wm, high, low, high2, low2, whigh, wlow, held, sems):
    both = 2 * HALF
    copies = pull(info_ref, held, sems, [(x, 0, both, 0, 0), (xx, 0, both, 1, 0), (s1, 0, both, 2, 0), (s1, both, both, 3, 0)])
    start_all(copies)
    split_into(whigh, wlow, [w, wp, wm])
    wait_all(copies)
    dense(info_ref, held, [high, high2], [low, low2])


def ready(info, sources, weights):
    columns = weights[0].shape[1]
    return pl.pallas_call(
        ready_kernel,
        out_shape=[pltpu.VMEM((ROWS, DEEP), bf16)] * 4 + [pltpu.VMEM((384, columns), bf16)] * 2,
        in_specs=[pl.BlockSpec(memory_space=pltpu.SMEM)] + [ANYWHERE] * 3 + [WHOLE] * 3,
        out_specs=[WHOLE] * 6,
        scratch_shapes=[pltpu.VMEM((8, ROWS, 128), f32), pltpu.SemaphoreType.DMA((4,))],
        compiler_params=pltpu.CompilerParams(vmem_limit_bytes=READY * MIB),
        cost_estimate=pl.CostEstimate(flops=4 * ROWS * DEEP, bytes_accessed=10 * MIB, transcendentals=0),
        name="ready",
    )(info, *sources, *weights)


def early_kernel(info_ref, s2, xp, xxp, xm, xxm, w2, high, low, whigh3, wlow3,
                 part_ref, ahigh_ref, alow_ref, whigh, wlow, held, bhigh, blow, sems):
    both = 2 * HALF
    copies = [
        pull(info_ref, held.at[j], sems.at[j], [
            (near_ref, 0, both, 0, 0), (far_ref, 0, both, 1, 0), (s2, 2 * j * both, both, 2, 0), (s2, (2 * j + 1) * both, both, 3, 0)
        ])
        for j, (near_ref, far_ref) in enumerate(((xp, xxp), (xm, xxm)))
    ]
    start_all(copies[0] + copies[1])
    whigh[0:384] = whigh3[...]
    wlow[0:384] = wlow3[...]
    split_into(whigh, wlow, [w2], 3)
    for j in range(3):
        if j:
            wait_all(copies[j - 1])
            dense(info_ref, held.at[j - 1], [bhigh.at[j - 1], ahigh_ref.at[j - 1]], [blow.at[j - 1], alow_ref.at[j - 1]])
        h, l = (high, low) if j == 0 else (bhigh.at[j - 1], blow.at[j - 1])
        for n in range(0, part_ref.shape[2], 256):
            part_ref[j, :, n : n + 256] = three(h[...], l[...], whigh[:, n : n + 256], wlow[:, n : n + 256])


def early(info, sources, w2, made):
    columns = w2.shape[1]
    return pl.pallas_call(
        early_kernel,
        out_shape=[
            pltpu.VMEM((3, ROWS, columns), f32),
            pltpu.VMEM((2, ROWS, DEEP), bf16),
            pltpu.VMEM((2, ROWS, DEEP), bf16),
            pltpu.VMEM((DEEP, columns), bf16),
            pltpu.VMEM((DEEP, columns), bf16),
        ],
        in_specs=[pl.BlockSpec(memory_space=pltpu.SMEM)] + [ANYWHERE] * 5 + [WHOLE] * 5,
        out_specs=[WHOLE] * 5,
        scratch_shapes=[
            pltpu.VMEM((2, 8, ROWS, 128), f32),
            pltpu.VMEM((2, ROWS, DEEP), bf16),
            pltpu.VMEM((2, ROWS, DEEP), bf16),
            pltpu.SemaphoreType.DMA((2, 4)),
        ],
        compiler_params=pltpu.CompilerParams(vmem_limit_bytes=EARLY * MIB),
        cost_estimate=pl.CostEstimate(flops=18 * ROWS * DEEP * columns, bytes_accessed=20 * MIB, transcendentals=0),
        name="early",
    )(info, *sources, w2, *(near(v) for v in made))


def finish(out_ref, rgap_ref, cgap_ref, n, total):
    tall = rgap_ref[...].reshape(-1, 128)
    for m in range(0, 256, 128):
        gap = tall + cgap_ref[:, n + m : n + m + 128]
        out_ref[:, 0, :, n + m : n + m + 128] = (total[:, m : m + 128] / gap).reshape(-1, 8, 128)


def late_kernel(info_ref, part_ref, high2, low2, ahigh_ref, alow_ref, wx, wxp, wxm, wx2, rgap_ref, cgap_ref,
                out_ref, whigh2, wlow2):
    chunk = pl.program_id(0)

    @pl.when(chunk == 0)
    def _():
        split_into(whigh2, wlow2, [wx, wxp, wxm, wx2])

    def work(h, l):
        for n in range(0, whigh2.shape[1], 256):
            cut = slice(n, n + 256)
            finish(out_ref, rgap_ref, cgap_ref, n, part_ref[chunk, :, cut] + three(h[...], l[...], whigh2[:, cut], wlow2[:, cut]))

    pl.when(chunk == 0)(lambda: work(high2, low2))
    pl.when(chunk > 0)(lambda: work(ahigh_ref.at[chunk - 1], alow_ref.at[chunk - 1]))


def late(info, part, own, others, weights, rgap, cgap, virtuals):
    columns = weights[0].shape[1]
    rows = lambda *shape: pl.BlockSpec((virtuals, 1, 8) + shape, lambda c, i: (0, i[4 + c], 0, 0))
    return pl.pallas_call(
        late_kernel,
        out_shape=[jax.ShapeDtypeStruct((virtuals, 4, 8, columns), f32)] + [pltpu.VMEM((DEEP, columns), bf16)] * 2,
        grid_spec=pltpu.PrefetchScalarGridSpec(
            num_scalar_prefetch=1,
            grid=(3,),
            in_specs=[WHOLE] * 9 + [rows(128), WHOLE],
            out_specs=[rows(columns), WHOLE, WHOLE],
        ),
        compiler_params=pltpu.CompilerParams(vmem_limit_bytes=LATE * MIB),
        cost_estimate=pl.CostEstimate(flops=18 * ROWS * DEEP * columns, bytes_accessed=24 * MIB, transcendentals=0),
        name="late",
    )(info, *(near(v) for v in (part, *own, *others)), *weights, rgap, cgap)


def last_kernel(info_ref, rest_ref, up, down, s3, whigh, wlow, whigh2, wlow2, rgap_ref, cgap_ref,
                out_ref, held, *scratch):
    *scratch, sems = scratch
    high, low, high2, low2 = (scratch[n : n + 2] for n in range(0, 8, 2))
    del rest_ref
    step = pl.program_id(0)
    pieces = []
    for ref, base, slot in ((up, 0, 0), (down, 0, 0), (s3, 0, 2), (s3, 2 * HALF, 2)):
        offset = HALF * (len(pieces) // 2 % 2)
        pieces += [(ref, base, HALF, slot, offset), (ref, base + HALF, HALF, slot + 1, offset)]
    copies = pull(info_ref, held, sems, pieces)

    half = out_ref.shape[0]

    def work(h):
        for n in range(0, whigh.shape[1], 256):
            cut = slice(n, n + 256)
            total = three(high[h][...], low[h][...], whigh[:, cut], wlow[:, cut])
            total += three(high2[h][...], low2[h][...], whigh2[:, cut], wlow2[:, cut])
            finish(out_ref, rgap_ref, cgap_ref, n, total)

    def gather(h):
        dense(info_ref, held, [high[h], high2[h]], [low[h], low2[h]], range(h * half, h * half + half))

    @pl.when(step == 0)
    def _():
        start_all(copies)
        wait_all(copies)
        gather(0)
        gather(1)
        work(0)

    @pl.when(step == 1)
    def _():
        work(1)


def last(info, rest, sources, weights, rgap, cgap, virtuals):
    columns = weights[0].shape[1]
    steps = 2
    rows = lambda *shape: pl.BlockSpec((virtuals // steps, 1, 8) + shape, lambda c, i: (c, i[7], 0, 0))
    return pl.pallas_call(
        last_kernel,
        out_shape=jax.ShapeDtypeStruct((virtuals, 4, 8, columns), f32),
        grid_spec=pltpu.PrefetchScalarGridSpec(
            num_scalar_prefetch=1,
            grid=(steps,),
            in_specs=[APART] + [ANYWHERE] * 3 + [WHOLE] * 4 + [rows(128), WHOLE],
            out_specs=rows(columns),
            scratch_shapes=[pltpu.VMEM((8, ROWS, 128), f32)]
            + [pltpu.VMEM((ROWS // steps, DEEP), bf16)] * 8
            + [pltpu.SemaphoreType.DMA((8,))],
        ),
        input_output_aliases={1: 0},
        compiler_params=pltpu.CompilerParams(vmem_limit_bytes=LAST * MIB),
        cost_estimate=pl.CostEstimate(flops=12 * ROWS * DEEP * columns, bytes_accessed=8 * MIB, transcendentals=0),
        name="last",
    )(info, rest, *sources, *(near(v) for v in weights), rgap, cgap)


def body(amplitudes, integrals, occ_energy, vir_energy):
    virtuals, own = amplitudes.shape[:2]
    depth = amplitudes.shape[2] * amplitudes.shape[3]
    columns = integrals.shape[1]
    y, xl, core, xh, z = (lax.axis_index(a) for a in AXES)

    info = jnp.stack(
        [xl * 2 + core, (1 - xl) * 2 + core, xl * 2 + 1 - core, (1 - xl) * 2 + 1 - core]
        + [y, (y + 3) % 4, (y + 1) % 4, (y + 2) % 4]
        + [z, (z + 3) % 4, (z + 1) % 4, (z + 2) % 4]
        + [xh, 1 - xh]
    ).astype(jnp.int32)
    gap = vir_energy[:, None] - occ_energy[None, :]
    row_gap = lax.dynamic_slice_in_dim(gap, (xh * 4 + z) * virtuals, virtuals)
    rgap = jnp.broadcast_to(row_gap.reshape(virtuals, 4, 8, 1), (virtuals, 4, 8, 128))
    start = ((y * 2 + xl) * 2 + core) * columns
    cgap = lax.dynamic_slice_in_dim(gap.reshape(-1), start, columns).reshape(1, columns)

    join = lambda *values: jnp.concatenate(values, axis=1)
    x = turn(amplitudes.transpose(1, 2, 3, 0).reshape(own, depth, virtuals))
    w = integrals

    wp, wm = hop(w, z=1), hop(w, z=3)
    xp, xm, xx = hop(x, y=1), hop(x, y=3), hop(x, xl=1)
    xx, wp, wm, info, rgap, cgap = lax.optimization_barrier((xx, wp, wm, info, rgap, cgap))
    xxp, xxm = hop(xx, y=1), hop(xx, y=3)
    w2, wx = hop(after(w, wp, wm), z=2), hop(after(w, xx), xh=1)
    s1 = hop(after(join(x, xx), xp, xm), core=1)
    high, low, high2, low2, whigh, wlow = ready(info, [x, xx, s1], [w, wp, wm])
    xxp, xxm, wlow = lax.optimization_barrier((xxp, xxm, wlow))
    wx, w2, xxp, xxm = lax.optimization_barrier((wx, w2, xxp, xxm))
    s2 = hop(join(xp, xxp, xm, xxm), core=1)
    up = hop(join(xp[:, :HALF], xxp[:, :HALF]), y=1)
    down = hop(join(xm[:, HALF:], xxm[:, HALF:]), y=3)
    wxp, wxm, wx2 = hop(wx, z=1), hop(wx, z=3), hop(w2, xh=1)

    part, ahigh, alow, whigh, wlow = early(info, [s2, xp, xxp, xm, xxm], w2, [high, low, whigh, wlow])
    up, down, wxp, wxm, wx2, wlow = lax.optimization_barrier((up, down, wxp, wxm, wx2, wlow))
    s3 = hop(join(up, down), core=1)
    out, whigh2, wlow2 = late(info, part, [high2, low2], [ahigh, alow], [wx, wxp, wxm, wx2], rgap, cgap, virtuals)
    out = last(info, out, [up, down, s3], [whigh, wlow, whigh2, wlow2], rgap, cgap, virtuals)
    return out.reshape(virtuals * 32, columns)


def solution(mesh):
    fine = Mesh(mesh.devices.reshape(SIZES), AXES)
    in_specs = (P(COL, ROW, None, None), P(COL, ROW), P(), P())
    return jax.shard_map(body, mesh=fine, in_specs=in_specs, out_specs=P(COL, ROW), check_vma=False)
```

```python
import functools

import jax
import jax.numpy as jnp
import numpy as np
from jax import lax
from jax.experimental import pallas as pl
from jax.experimental.pallas import tpu as pltpu
from jax.sharding import Mesh, PartitionSpec as P

ROW = ("y", "xl", "core")
COL = ("xh", "z")
AXES = ROW + COL
SIZES = (4, 2, 2, 2, 4)
f32, bf16 = jnp.float32, jnp.bfloat16
MIB = 1 << 20
READY, EARLY, LATE, LAST = 20, 24, 24, 24
TURN_FLOPS = 1 << 20
HALF = 64


def hop(value, **move):
    pairs = []
    for source in range(int(np.prod(SIZES))):
        place = list(np.unravel_index(source, SIZES))
        for axis, step in move.items():
            k = AXES.index(axis)
            place[k] = (place[k] + step) % SIZES[k]
        pairs.append((source, int(np.ravel_multi_index(place, SIZES))))
    return lax.ppermute(value, AXES, pairs)


def after(value, *needed):
    return lax.optimization_barrier((value,) + needed)[0]


def split(value):
    high = value.astype(bf16)
    return high, (value - high.astype(f32)).astype(bf16)


def turn_kernel(amp_ref, out_ref):
    for n in range(out_ref.shape[0]):
        lanes = slice(n * 128, n * 128 + 128)
        both = jnp.concatenate([amp_ref[0, lanes], amp_ref[1, lanes]], axis=1)
        out_ref[n] = both.T


def turn(amp):
    two, depth, width = amp.shape
    return pl.pallas_call(
        turn_kernel,
        out_shape=jax.ShapeDtypeStruct((depth // 128, two * width, 128), f32),
        in_specs=[pl.BlockSpec(memory_space=pltpu.VMEM)],
        out_specs=pl.BlockSpec(memory_space=pltpu.VMEM),
        cost_estimate=pl.CostEstimate(flops=TURN_FLOPS, bytes_accessed=2 * MIB, transcendentals=0),
        name="turn",
    )(amp)


def dense(info_ref, held, high_refs, low_refs, rows=range(64)):
    width = held.shape[1] // 8
    for h in range(2):
        base = info_ref[12 + h] * 4
        for k in range(4):
            block = held.at[base + info_ref[8 + k]]
            for a in range(rows.start, rows.stop, 2):
                value = jnp.concatenate([block[pl.ds(a + b, 8, stride=width), :] for b in range(2)], axis=0)
                high, low = split(value)
                row = (a - rows.start) * 8
                high_refs[h][row : row + 16, k * 128 : k * 128 + 128] = high
                low_refs[h][row : row + 16, k * 128 : k * 128 + 128] = low


def three(high, low, whigh, wlow):
    total = jnp.dot(high, whigh, preferred_element_type=f32)
    total += jnp.dot(high, wlow, preferred_element_type=f32)
    return total + jnp.dot(low, whigh, preferred_element_type=f32)


def pull(info_ref, held, sems, pieces):
    copies = []
    for n, (ref, start, rows, slot, offset) in enumerate(pieces):
        row = pl.multiple_of(info_ref[slot] * (2 * HALF) + offset, 8)
        copies.append(pltpu.make_async_copy(ref.at[:, pl.ds(start, rows)], held.at[:, pl.ds(row, rows)], sems.at[n]))
    return copies


def start_all(copies):
    for copy in copies:
        copy.start()


def wait_all(copies):
    for copy in copies:
        copy.wait()


def split_into(high_ref, low_ref, pieces, first=0):
    for n, ref in enumerate(pieces):
        row = (first + n) * 128
        high_ref[row : row + 128], low_ref[row : row + 128] = split(ref[...])


WHOLE = pl.BlockSpec(memory_space=pltpu.VMEM)
APART = pl.BlockSpec(memory_space=pltpu.HBM)
ANYWHERE = pl.BlockSpec(memory_space=pl.ANY)
ROWS = 8 * HALF
DEEP = 512
near = lambda value: pltpu.with_memory_space_constraint(value, pltpu.VMEM)


def ready_kernel(info_ref, x, xx, s1, w, wp, wm, high, low, high2, low2, whigh, wlow, held, sems):
    both = 2 * HALF
    copies = pull(info_ref, held, sems, [(x, 0, both, 0, 0), (xx, 0, both, 1, 0), (s1, 0, both, 2, 0), (s1, both, both, 3, 0)])
    start_all(copies)
    split_into(whigh, wlow, [w, wp, wm])
    wait_all(copies)
    dense(info_ref, held, [high, high2], [low, low2])


def ready(info, sources, weights):
    columns = weights[0].shape[1]
    return pl.pallas_call(
        ready_kernel,
        out_shape=[pltpu.VMEM((ROWS, DEEP), bf16)] * 4 + [pltpu.VMEM((384, columns), bf16)] * 2,
        in_specs=[pl.BlockSpec(memory_space=pltpu.SMEM)] + [ANYWHERE] * 3 + [WHOLE] * 3,
        out_specs=[WHOLE] * 6,
        scratch_shapes=[pltpu.VMEM((8, ROWS, 128), f32), pltpu.SemaphoreType.DMA((4,))],
        compiler_params=pltpu.CompilerParams(vmem_limit_bytes=READY * MIB),
        cost_estimate=pl.CostEstimate(flops=4 * ROWS * DEEP, bytes_accessed=10 * MIB, transcendentals=0),
        name="ready",
    )(info, *sources, *weights)


def early_kernel(info_ref, s2, xp, xxp, xm, xxm, w2, high, low, whigh3, wlow3,
                 part_ref, ahigh_ref, alow_ref, whigh, wlow, held, bhigh, blow, sems):
    both = 2 * HALF
    copies = [
        pull(info_ref, held.at[j], sems.at[j], [
            (near_ref, 0, both, 0, 0), (far_ref, 0, both, 1, 0), (s2, (2 * j + 2) * both, both, 2, 0), (s2, (2 * j + 3) * both, both, 3, 0)
        ])
        for j, (near_ref, far_ref) in enumerate(((xp, xxp), (xm, xxm)))
    ]
    start_all(copies[0] + copies[1])
    whigh[0:384] = whigh3[...]
    wlow[0:384] = wlow3[...]
    split_into(whigh, wlow, [w2], 3)
    for j in range(3):
        if j:
            wait_all(copies[j - 1])
            dense(info_ref, held.at[j - 1], [bhigh.at[j - 1], ahigh_ref.at[j - 1]], [blow.at[j - 1], alow_ref.at[j - 1]])
        h, l = (high, low) if j == 0 else (bhigh.at[j - 1], blow.at[j - 1])
        for n in range(0, part_ref.shape[2], 256):
            part_ref[j, :, n : n + 256] = three(h[...], l[...], whigh[:, n : n + 256], wlow[:, n : n + 256])


def early(info, sources, w2, made):
    columns = w2.shape[1]
    return pl.pallas_call(
        early_kernel,
        out_shape=[
            pltpu.VMEM((3, ROWS, columns), f32),
            pltpu.VMEM((2, ROWS, DEEP), bf16),
            pltpu.VMEM((2, ROWS, DEEP), bf16),
            pltpu.VMEM((DEEP, columns), bf16),
            pltpu.VMEM((DEEP, columns), bf16),
        ],
        in_specs=[pl.BlockSpec(memory_space=pltpu.SMEM)] + [ANYWHERE] * 5 + [WHOLE] * 5,
        out_specs=[WHOLE] * 5,
        scratch_shapes=[
            pltpu.VMEM((2, 8, ROWS, 128), f32),
            pltpu.VMEM((2, ROWS, DEEP), bf16),
            pltpu.VMEM((2, ROWS, DEEP), bf16),
            pltpu.SemaphoreType.DMA((2, 4)),
        ],
        compiler_params=pltpu.CompilerParams(vmem_limit_bytes=EARLY * MIB),
        cost_estimate=pl.CostEstimate(flops=18 * ROWS * DEEP * columns, bytes_accessed=20 * MIB, transcendentals=0),
        name="early",
    )(info, *sources, w2, *(near(v) for v in made))


def finish(out_ref, rgap_ref, cgap_ref, n, total):
    tall = rgap_ref[...].reshape(-1, 128)
    for m in range(0, 256, 128):
        gap = tall + cgap_ref[:, n + m : n + m + 128]
        out_ref[:, 0, :, n + m : n + m + 128] = (total[:, m : m + 128] / gap).reshape(-1, 8, 128)


def late_kernel(info_ref, part_ref, high2, low2, ahigh_ref, alow_ref, wx, wxp, wxm, wx2, rgap_ref, cgap_ref,
                out_ref, whigh2, wlow2):
    chunk = pl.program_id(0)

    @pl.when(chunk == 0)
    def _():
        split_into(whigh2, wlow2, [wx, wxp, wxm, wx2])

    def work(h, l):
        for n in range(0, whigh2.shape[1], 256):
            cut = slice(n, n + 256)
            finish(out_ref, rgap_ref, cgap_ref, n, part_ref[chunk, :, cut] + three(h[...], l[...], whigh2[:, cut], wlow2[:, cut]))

    pl.when(chunk == 0)(lambda: work(high2, low2))
    pl.when(chunk > 0)(lambda: work(ahigh_ref.at[chunk - 1], alow_ref.at[chunk - 1]))


def late(info, part, own, others, weights, rgap, cgap, virtuals):
    columns = weights[0].shape[1]
    rows = lambda *shape: pl.BlockSpec((virtuals, 1, 8) + shape, lambda c, i: (0, i[4 + c], 0, 0))
    return pl.pallas_call(
        late_kernel,
        out_shape=[jax.ShapeDtypeStruct((virtuals, 4, 8, columns), f32)] + [pltpu.VMEM((DEEP, columns), bf16)] * 2,
        grid_spec=pltpu.PrefetchScalarGridSpec(
            num_scalar_prefetch=1,
            grid=(3,),
            in_specs=[WHOLE] * 9 + [rows(128), WHOLE],
            out_specs=[rows(columns), WHOLE, WHOLE],
        ),
        compiler_params=pltpu.CompilerParams(vmem_limit_bytes=LATE * MIB),
        cost_estimate=pl.CostEstimate(flops=18 * ROWS * DEEP * columns, bytes_accessed=24 * MIB, transcendentals=0),
        name="late",
    )(info, *(near(v) for v in (part, *own, *others)), *weights, rgap, cgap)


def last_kernel(info_ref, rest_ref, up, down, s3, whigh, wlow, whigh2, wlow2, rgap_ref, cgap_ref,
                out_ref, held, *scratch):
    *scratch, sems = scratch
    high, low, high2, low2 = (scratch[n : n + 2] for n in range(0, 8, 2))
    del rest_ref
    step = pl.program_id(0)
    pieces = []
    for ref, base, slot in ((up, 0, 0), (down, 0, 0), (s3, 0, 2), (s3, 2 * HALF, 2)):
        offset = HALF * (len(pieces) // 2 % 2)
        pieces += [(ref, base, HALF, slot, offset), (ref, base + HALF, HALF, slot + 1, offset)]
    copies = pull(info_ref, held, sems, pieces)

    half = out_ref.shape[0]

    def work(h):
        for n in range(0, whigh.shape[1], 256):
            cut = slice(n, n + 256)
            total = three(high[h][...], low[h][...], whigh[:, cut], wlow[:, cut])
            total += three(high2[h][...], low2[h][...], whigh2[:, cut], wlow2[:, cut])
            finish(out_ref, rgap_ref, cgap_ref, n, total)

    def gather(h):
        dense(info_ref, held, [high[h], high2[h]], [low[h], low2[h]], range(h * half, h * half + half))

    @pl.when(step == 0)
    def _():
        start_all(copies)
        wait_all(copies)
        gather(0)
        gather(1)
        work(0)

    @pl.when(step == 1)
    def _():
        work(1)


def last(info, rest, sources, weights, rgap, cgap, virtuals):
    columns = weights[0].shape[1]
    steps = 2
    rows = lambda *shape: pl.BlockSpec((virtuals // steps, 1, 8) + shape, lambda c, i: (c, i[7], 0, 0))
    return pl.pallas_call(
        last_kernel,
        out_shape=jax.ShapeDtypeStruct((virtuals, 4, 8, columns), f32),
        grid_spec=pltpu.PrefetchScalarGridSpec(
            num_scalar_prefetch=1,
            grid=(steps,),
            in_specs=[APART] + [ANYWHERE] * 3 + [WHOLE] * 4 + [rows(128), WHOLE],
            out_specs=rows(columns),
            scratch_shapes=[pltpu.VMEM((8, ROWS, 128), f32)]
            + [pltpu.VMEM((ROWS // steps, DEEP), bf16)] * 8
            + [pltpu.SemaphoreType.DMA((8,))],
        ),
        input_output_aliases={1: 0},
        compiler_params=pltpu.CompilerParams(vmem_limit_bytes=LAST * MIB),
        cost_estimate=pl.CostEstimate(flops=12 * ROWS * DEEP * columns, bytes_accessed=8 * MIB, transcendentals=0),
        name="last",
    )(info, rest, *sources, *(near(v) for v in weights), rgap, cgap)


def body(amplitudes, integrals, occ_energy, vir_energy):
    virtuals, own = amplitudes.shape[:2]
    depth = amplitudes.shape[2] * amplitudes.shape[3]
    columns = integrals.shape[1]
    y, xl, core, xh, z = (lax.axis_index(a) for a in AXES)

    info = jnp.stack(
        [xl * 2 + core, (1 - xl) * 2 + core, xl * 2 + 1 - core, (1 - xl) * 2 + 1 - core]
        + [y, (y + 3) % 4, (y + 1) % 4, (y + 2) % 4]
        + [z, (z + 3) % 4, (z + 1) % 4, (z + 2) % 4]
        + [xh, 1 - xh]
    ).astype(jnp.int32)
    gap = vir_energy[:, None] - occ_energy[None, :]
    row_gap = lax.dynamic_slice_in_dim(gap, (xh * 4 + z) * virtuals, virtuals)
    rgap = jnp.broadcast_to(row_gap.reshape(virtuals, 4, 8, 1), (virtuals, 4, 8, 128))
    start = ((y * 2 + xl) * 2 + core) * columns
    cgap = lax.dynamic_slice_in_dim(gap.reshape(-1), start, columns).reshape(1, columns)

    join = lambda *values: jnp.concatenate(values, axis=1)
    x = turn(amplitudes.transpose(1, 2, 3, 0).reshape(own, depth, virtuals))
    w = integrals

    wp, wm = hop(w, z=1), hop(w, z=3)
    xp, xm, xx = hop(x, y=1), hop(x, y=3), hop(x, xl=1)
    xx, wp, wm, info, rgap, cgap = lax.optimization_barrier((xx, wp, wm, info, rgap, cgap))
    xxp, xxm = hop(xx, y=1), hop(xx, y=3)
    w2, wx = hop(after(w, wp, wm, xp), z=2), hop(after(w, xx, xm), xh=1)
    xxp, xxm = lax.optimization_barrier((xxp, xxm))
    wx, w2, xxp, xxm = lax.optimization_barrier((wx, w2, xxp, xxm))
    s2 = hop(join(x, xx, xp, xxp, xm, xxm), core=1)
    up = hop(join(xp[:, :HALF], xxp[:, :HALF]), y=1)
    down = hop(join(xm[:, HALF:], xxm[:, HALF:]), y=3)
    wxp, wxm, wx2 = hop(wx, z=1), hop(wx, z=3), hop(w2, xh=1)

    high, low, high2, low2, whigh, wlow = ready(info, [x, xx, s2], [w, wp, wm])
    part, ahigh, alow, whigh, wlow = early(info, [s2, xp, xxp, xm, xxm], w2, [high, low, whigh, wlow])
    up, down, wxp, wxm, wx2, wlow = lax.optimization_barrier((up, down, wxp, wxm, wx2, wlow))
    s3 = hop(join(up, down), core=1)
    out, whigh2, wlow2 = late(info, part, [high2, low2], [ahigh, alow], [wx, wxp, wxm, wx2], rgap, cgap, virtuals)
    out = last(info, out, [up, down, s3], [whigh, wlow, whigh2, wlow2], rgap, cgap, virtuals)
    return out.reshape(virtuals * 32, columns)


def solution(mesh):
    fine = Mesh(mesh.devices.reshape(SIZES), AXES)
    in_specs = (P(COL, ROW, None, None), P(COL, ROW), P(), P())
    return jax.shard_map(body, mesh=fine, in_specs=in_specs, out_specs=P(COL, ROW), check_vma=False)
```

```python
import functools

import jax
import jax.numpy as jnp
import numpy as np
from jax import lax
from jax.experimental import pallas as pl
from jax.experimental.pallas import tpu as pltpu
from jax.sharding import Mesh, PartitionSpec as P

ROW = ("y", "xl", "core")
COL = ("xh", "z")
AXES = ROW + COL
SIZES = (4, 2, 2, 2, 4)
f32, bf16 = jnp.float32, jnp.bfloat16
MIB = 1 << 20
READY, EARLY, LATE, LAST = 20, 24, 24, 24
TURN_FLOPS = 1 << 20
HALF = 64


def hop(value, **move):
    pairs = []
    for source in range(int(np.prod(SIZES))):
        place = list(np.unravel_index(source, SIZES))
        for axis, step in move.items():
            k = AXES.index(axis)
            place[k] = (place[k] + step) % SIZES[k]
        pairs.append((source, int(np.ravel_multi_index(place, SIZES))))
    return lax.ppermute(value, AXES, pairs)


def after(value, *needed):
    return lax.optimization_barrier((value,) + needed)[0]


def split(value):
    high = value.astype(bf16)
    return high, (value - high.astype(f32)).astype(bf16)


def turn_kernel(amp_ref, out_ref):
    for n in range(out_ref.shape[0]):
        lanes = slice(n * 128, n * 128 + 128)
        both = jnp.concatenate([amp_ref[0, lanes], amp_ref[1, lanes]], axis=1)
        out_ref[n] = both.T


def turn(amp):
    two, depth, width = amp.shape
    return pl.pallas_call(
        turn_kernel,
        out_shape=jax.ShapeDtypeStruct((depth // 128, two * width, 128), f32),
        in_specs=[pl.BlockSpec(memory_space=pltpu.VMEM)],
        out_specs=pl.BlockSpec(memory_space=pltpu.VMEM),
        cost_estimate=pl.CostEstimate(flops=TURN_FLOPS, bytes_accessed=2 * MIB, transcendentals=0),
        name="turn",
    )(amp)


def dense(info_ref, held, high_refs, low_refs, rows=range(64)):
    width = held.shape[1] // 8
    for h in range(2):
        base = info_ref[12 + h] * 4
        for k in range(4):
            block = held.at[base + info_ref[8 + k]]
            for a in range(rows.start, rows.stop, 2):
                value = jnp.concatenate([block[pl.ds(a + b, 8, stride=width), :] for b in range(2)], axis=0)
                high, low = split(value)
                row = (a - rows.start) * 8
                high_refs[h][row : row + 16, k * 128 : k * 128 + 128] = high
                low_refs[h][row : row + 16, k * 128 : k * 128 + 128] = low


def three(high, low, whigh, wlow):
    total = jnp.dot(high, whigh, preferred_element_type=f32)
    total += jnp.dot(high, wlow, preferred_element_type=f32)
    return total + jnp.dot(low, whigh, preferred_element_type=f32)


def pull(info_ref, held, sems, pieces):
    copies = []
    for n, (ref, start, rows, slot, offset) in enumerate(pieces):
        row = pl.multiple_of(info_ref[slot] * (2 * HALF) + offset, 8)
        copies.append(pltpu.make_async_copy(ref.at[:, pl.ds(start, rows)], held.at[:, pl.ds(row, rows)], sems.at[n]))
    return copies


def start_all(copies):
    for copy in copies:
        copy.start()


def wait_all(copies):
    for copy in copies:
        copy.wait()


def split_into(high_ref, low_ref, pieces, first=0):
    for n, ref in enumerate(pieces):
        row = (first + n) * 128
        high_ref[row : row + 128], low_ref[row : row + 128] = split(ref[...])


WHOLE = pl.BlockSpec(memory_space=pltpu.VMEM)
APART = pl.BlockSpec(memory_space=pltpu.HBM)
ANYWHERE = pl.BlockSpec(memory_space=pl.ANY)
ROWS = 8 * HALF
DEEP = 512
near = lambda value: pltpu.with_memory_space_constraint(value, pltpu.VMEM)


def ready_kernel(info_ref, x, xx, s1, w, wp, wm, high, low, high2, low2, whigh, wlow, held, sems):
    both = 2 * HALF
    copies = pull(info_ref, held, sems, [(x, 0, both, 0, 0), (xx, 0, both, 1, 0), (s1, 0, both, 2, 0), (s1, both, both, 3, 0)])
    start_all(copies)
    split_into(whigh, wlow, [w, wp, wm])
    wait_all(copies)
    dense(info_ref, held, [high, high2], [low, low2])


def ready(info, sources, weights):
    columns = weights[0].shape[1]
    return pl.pallas_call(
        ready_kernel,
        out_shape=[pltpu.VMEM((ROWS, DEEP), bf16)] * 4 + [pltpu.VMEM((384, columns), bf16)] * 2,
        in_specs=[pl.BlockSpec(memory_space=pltpu.SMEM)] + [ANYWHERE] * 3 + [WHOLE] * 3,
        out_specs=[WHOLE] * 6,
        scratch_shapes=[pltpu.VMEM((8, ROWS, 128), f32), pltpu.SemaphoreType.DMA((4,))],
        compiler_params=pltpu.CompilerParams(vmem_limit_bytes=READY * MIB),
        cost_estimate=pl.CostEstimate(flops=4 * ROWS * DEEP, bytes_accessed=10 * MIB, transcendentals=0),
        name="ready",
    )(info, *sources, *weights)


def early_kernel(info_ref, s2, xp, xxp, xm, xxm, w2, high, low, whigh3, wlow3,
                 part_ref, ahigh_ref, alow_ref, whigh, wlow, held, bhigh, blow, sems):
    both = 2 * HALF
    copies = [
        pull(info_ref, held.at[j], sems.at[j], [
            (near_ref, 0, both, 0, 0), (far_ref, 0, both, 1, 0), (s2, (2 * j + 2) * both, both, 2, 0), (s2, (2 * j + 3) * both, both, 3, 0)
        ])
        for j, (near_ref, far_ref) in enumerate(((xp, xxp), (xm, xxm)))
    ]
    start_all(copies[0] + copies[1])
    whigh[0:384] = whigh3[...]
    wlow[0:384] = wlow3[...]
    split_into(whigh, wlow, [w2], 3)
    for j in range(3):
        if j:
            wait_all(copies[j - 1])
            dense(info_ref, held.at[j - 1], [bhigh.at[j - 1], ahigh_ref.at[j - 1]], [blow.at[j - 1], alow_ref.at[j - 1]])
        h, l = (high, low) if j == 0 else (bhigh.at[j - 1], blow.at[j - 1])
        for n in range(0, part_ref.shape[2], 256):
            part_ref[j, :, n : n + 256] = three(h[...], l[...], whigh[:, n : n + 256], wlow[:, n : n + 256])


def early(info, sources, w2, made):
    columns = w2.shape[1]
    return pl.pallas_call(
        early_kernel,
        out_shape=[
            pltpu.VMEM((3, ROWS, columns), f32),
            pltpu.VMEM((2, ROWS, DEEP), bf16),
            pltpu.VMEM((2, ROWS, DEEP), bf16),
            pltpu.VMEM((DEEP, columns), bf16),
            pltpu.VMEM((DEEP, columns), bf16),
        ],
        in_specs=[pl.BlockSpec(memory_space=pltpu.SMEM)] + [ANYWHERE] * 5 + [WHOLE] * 5,
        out_specs=[WHOLE] * 5,
        scratch_shapes=[
            pltpu.VMEM((2, 8, ROWS, 128), f32),
            pltpu.VMEM((2, ROWS, DEEP), bf16),
            pltpu.VMEM((2, ROWS, DEEP), bf16),
            pltpu.SemaphoreType.DMA((2, 4)),
        ],
        compiler_params=pltpu.CompilerParams(vmem_limit_bytes=EARLY * MIB),
        cost_estimate=pl.CostEstimate(flops=18 * ROWS * DEEP * columns, bytes_accessed=20 * MIB, transcendentals=0),
        name="early",
    )(info, *sources, w2, *(near(v) for v in made))


def finish(out_ref, rgap_ref, cgap_ref, n, total):
    tall = rgap_ref[...].reshape(-1, 128)
    for m in range(0, 256, 128):
        gap = tall + cgap_ref[:, n + m : n + m + 128]
        out_ref[:, 0, :, n + m : n + m + 128] = (total[:, m : m + 128] / gap).reshape(-1, 8, 128)


def late_kernel(info_ref, part_ref, high2, low2, ahigh_ref, alow_ref, wx, wxp, wxm, wx2, rgap_ref, cgap_ref,
                out_ref, whigh2, wlow2):
    chunk = pl.program_id(0)

    @pl.when(chunk == 0)
    def _():
        split_into(whigh2, wlow2, [wx, wxp, wxm, wx2])

    def work(h, l):
        for n in range(0, whigh2.shape[1], 256):
            cut = slice(n, n + 256)
            finish(out_ref, rgap_ref, cgap_ref, n, part_ref[chunk, :, cut] + three(h[...], l[...], whigh2[:, cut], wlow2[:, cut]))

    pl.when(chunk == 0)(lambda: work(high2, low2))
    pl.when(chunk > 0)(lambda: work(ahigh_ref.at[chunk - 1], alow_ref.at[chunk - 1]))


def late(info, part, own, others, weights, rgap, cgap, virtuals):
    columns = weights[0].shape[1]
    rows = lambda *shape: pl.BlockSpec((virtuals, 1, 8) + shape, lambda c, i: (0, i[4 + c], 0, 0))
    return pl.pallas_call(
        late_kernel,
        out_shape=[jax.ShapeDtypeStruct((virtuals, 4, 8, columns), f32)] + [pltpu.VMEM((DEEP, columns), bf16)] * 2,
        grid_spec=pltpu.PrefetchScalarGridSpec(
            num_scalar_prefetch=1,
            grid=(3,),
            in_specs=[WHOLE] * 9 + [rows(128), WHOLE],
            out_specs=[rows(columns), WHOLE, WHOLE],
        ),
        compiler_params=pltpu.CompilerParams(vmem_limit_bytes=LATE * MIB),
        cost_estimate=pl.CostEstimate(flops=18 * ROWS * DEEP * columns, bytes_accessed=24 * MIB, transcendentals=0),
        name="late",
    )(info, *(near(v) for v in (part, *own, *others)), *weights, rgap, cgap)


def last_kernel(info_ref, rest_ref, up, down, s3, whigh, wlow, whigh2, wlow2, rgap_ref, cgap_ref,
                out_ref, held, *scratch):
    *scratch, sems = scratch
    high, low, high2, low2 = (scratch[n : n + 2] for n in range(0, 8, 2))
    del rest_ref
    step = pl.program_id(0)
    pieces = []
    for ref, base, slot in ((up, 0, 0), (down, 0, 0), (s3, 0, 2), (s3, 2 * HALF, 2)):
        offset = HALF * (len(pieces) // 2 % 2)
        pieces += [(ref, base, HALF, slot, offset), (ref, base + HALF, HALF, slot + 1, offset)]
    copies = pull(info_ref, held, sems, pieces)

    half = out_ref.shape[0]

    def work(h):
        for n in range(0, whigh.shape[1], 256):
            cut = slice(n, n + 256)
            total = three(high[h][...], low[h][...], whigh[:, cut], wlow[:, cut])
            total += three(high2[h][...], low2[h][...], whigh2[:, cut], wlow2[:, cut])
            finish(out_ref, rgap_ref, cgap_ref, n, total)

    def gather(h):
        dense(info_ref, held, [high[h], high2[h]], [low[h], low2[h]], range(h * half, h * half + half))

    @pl.when(step == 0)
    def _():
        start_all(copies)
        wait_all(copies)
        gather(0)
        gather(1)
        work(0)

    @pl.when(step == 1)
    def _():
        work(1)


def last(info, rest, sources, weights, rgap, cgap, virtuals):
    columns = weights[0].shape[1]
    steps = 2
    rows = lambda *shape: pl.BlockSpec((virtuals // steps, 1, 8) + shape, lambda c, i: (c, i[7], 0, 0))
    return pl.pallas_call(
        last_kernel,
        out_shape=jax.ShapeDtypeStruct((virtuals, 4, 8, columns), f32),
        grid_spec=pltpu.PrefetchScalarGridSpec(
            num_scalar_prefetch=1,
            grid=(steps,),
            in_specs=[APART] + [ANYWHERE] * 3 + [WHOLE] * 4 + [rows(128), WHOLE],
            out_specs=rows(columns),
            scratch_shapes=[pltpu.VMEM((8, ROWS, 128), f32)]
            + [pltpu.VMEM((ROWS // steps, DEEP), bf16)] * 8
            + [pltpu.SemaphoreType.DMA((8,))],
        ),
        input_output_aliases={1: 0},
        compiler_params=pltpu.CompilerParams(vmem_limit_bytes=LAST * MIB),
        cost_estimate=pl.CostEstimate(flops=12 * ROWS * DEEP * columns, bytes_accessed=8 * MIB, transcendentals=0),
        name="last",
    )(info, rest, *sources, *(near(v) for v in weights), rgap, cgap)


def body(amplitudes, integrals, occ_energy, vir_energy):
    virtuals, own = amplitudes.shape[:2]
    depth = amplitudes.shape[2] * amplitudes.shape[3]
    columns = integrals.shape[1]
    y, xl, core, xh, z = (lax.axis_index(a) for a in AXES)

    info = jnp.stack(
        [xl * 2 + core, (1 - xl) * 2 + core, xl * 2 + 1 - core, (1 - xl) * 2 + 1 - core]
        + [y, (y + 3) % 4, (y + 1) % 4, (y + 2) % 4]
        + [z, (z + 3) % 4, (z + 1) % 4, (z + 2) % 4]
        + [xh, 1 - xh]
    ).astype(jnp.int32)
    gap = vir_energy[:, None] - occ_energy[None, :]
    row_gap = lax.dynamic_slice_in_dim(gap, (xh * 4 + z) * virtuals, virtuals)
    rgap = jnp.broadcast_to(row_gap.reshape(virtuals, 4, 8, 1), (virtuals, 4, 8, 128))
    start = ((y * 2 + xl) * 2 + core) * columns
    cgap = lax.dynamic_slice_in_dim(gap.reshape(-1), start, columns).reshape(1, columns)

    join = lambda *values: jnp.concatenate(values, axis=1)
    x = turn(amplitudes.transpose(1, 2, 3, 0).reshape(own, depth, virtuals))
    w = integrals

    wp, wm = hop(w, z=1), hop(w, z=3)
    xp, xm, xx = hop(x, y=1), hop(x, y=3), hop(x, xl=1)
    xx, info, rgap, cgap = lax.optimization_barrier((xx, info, rgap, cgap))
    xxp, xxm = hop(xx, y=1), hop(xx, y=3)
    w2, wx = hop(after(w, wp, wm, xp, xm), z=2), hop(after(w, xx, xp, xm, wp, wm), xh=1)
    xxp, xxm = lax.optimization_barrier((xxp, xxm))
    wx, w2, xxp, xxm = lax.optimization_barrier((wx, w2, xxp, xxm))
    s2 = hop(join(x, xx, xp, xxp, xm, xxm), core=1)
    up = hop(join(xp[:, :HALF], xxp[:, :HALF]), y=1)
    down = hop(join(xm[:, HALF:], xxm[:, HALF:]), y=3)
    wxp, wxm, wx2 = hop(wx, z=1), hop(wx, z=3), hop(w2, xh=1)

    high, low, high2, low2, whigh, wlow = ready(info, [x, xx, s2], [w, wp, wm])
    part, ahigh, alow, whigh, wlow = early(info, [s2, xp, xxp, xm, xxm], w2, [high, low, whigh, wlow])
    up, down, wxp, wxm, wx2, wlow = lax.optimization_barrier((up, down, wxp, wxm, wx2, wlow))
    s3 = hop(join(up, down), core=1)
    out, whigh2, wlow2 = late(info, part, [high2, low2], [ahigh, alow], [wx, wxp, wxm, wx2], rgap, cgap, virtuals)
    out = last(info, out, [up, down, s3], [whigh, wlow, whigh2, wlow2], rgap, cgap, virtuals)
    return out.reshape(virtuals * 32, columns)


def solution(mesh):
    fine = Mesh(mesh.devices.reshape(SIZES), AXES)
    in_specs = (P(COL, ROW, None, None), P(COL, ROW), P(), P())
    return jax.shard_map(body, mesh=fine, in_specs=in_specs, out_specs=P(COL, ROW), check_vma=False)
```

```python
import functools

import jax
import jax.numpy as jnp
import numpy as np
from jax import lax
from jax.experimental import pallas as pl
from jax.experimental.pallas import tpu as pltpu
from jax.sharding import Mesh, PartitionSpec as P

ROW = ("y", "xl", "core")
COL = ("xh", "z")
AXES = ROW + COL
SIZES = (4, 2, 2, 2, 4)
f32, bf16 = jnp.float32, jnp.bfloat16
MIB = 1 << 20
READY, EARLY, LATE, LAST = 20, 24, 24, 24
TURN_FLOPS = 1 << 20
HALF = 64


def hop(value, **move):
    pairs = []
    for source in range(int(np.prod(SIZES))):
        place = list(np.unravel_index(source, SIZES))
        for axis, step in move.items():
            k = AXES.index(axis)
            place[k] = (place[k] + step) % SIZES[k]
        pairs.append((source, int(np.ravel_multi_index(place, SIZES))))
    return lax.ppermute(value, AXES, pairs)


def after(value, *needed):
    return lax.optimization_barrier((value,) + needed)[0]


def split(value):
    high = value.astype(bf16)
    return high, (value - high.astype(f32)).astype(bf16)


def turn_kernel(amp_ref, out_ref):
    for n in range(out_ref.shape[0]):
        lanes = slice(n * 128, n * 128 + 128)
        both = jnp.concatenate([amp_ref[0, lanes], amp_ref[1, lanes]], axis=1)
        out_ref[n] = both.T


def turn(amp):
    two, depth, width = amp.shape
    return pl.pallas_call(
        turn_kernel,
        out_shape=jax.ShapeDtypeStruct((depth // 128, two * width, 128), f32),
        in_specs=[pl.BlockSpec(memory_space=pltpu.VMEM)],
        out_specs=pl.BlockSpec(memory_space=pltpu.VMEM),
        cost_estimate=pl.CostEstimate(flops=TURN_FLOPS, bytes_accessed=2 * MIB, transcendentals=0),
        name="turn",
    )(amp)


def dense(info_ref, held, high_refs, low_refs, rows=range(64)):
    width = held.shape[1] // 8
    for h in range(2):
        base = info_ref[12 + h] * 4
        for k in range(4):
            block = held.at[base + info_ref[8 + k]]
            for a in range(rows.start, rows.stop, 2):
                value = jnp.concatenate([block[pl.ds(a + b, 8, stride=width), :] for b in range(2)], axis=0)
                high, low = split(value)
                row = (a - rows.start) * 8
                high_refs[h][row : row + 16, k * 128 : k * 128 + 128] = high
                low_refs[h][row : row + 16, k * 128 : k * 128 + 128] = low


def three(high, low, whigh, wlow):
    total = jnp.dot(high, whigh, preferred_element_type=f32)
    total += jnp.dot(high, wlow, preferred_element_type=f32)
    return total + jnp.dot(low, whigh, preferred_element_type=f32)


def pull(info_ref, held, sems, pieces):
    copies = []
    for n, (ref, start, rows, slot, offset) in enumerate(pieces):
        row = pl.multiple_of(info_ref[slot] * (2 * HALF) + offset, 8)
        copies.append(pltpu.make_async_copy(ref.at[:, pl.ds(start, rows)], held.at[:, pl.ds(row, rows)], sems.at[n]))
    return copies


def start_all(copies):
    for copy in copies:
        copy.start()


def wait_all(copies):
    for copy in copies:
        copy.wait()


def split_into(high_ref, low_ref, pieces, first=0):
    for n, ref in enumerate(pieces):
        row = (first + n) * 128
        high_ref[row : row + 128], low_ref[row : row + 128] = split(ref[...])


WHOLE = pl.BlockSpec(memory_space=pltpu.VMEM)
APART = pl.BlockSpec(memory_space=pltpu.HBM)
ANYWHERE = pl.BlockSpec(memory_space=pl.ANY)
ROWS = 8 * HALF
DEEP = 512
near = lambda value: pltpu.with_memory_space_constraint(value, pltpu.VMEM)


def ready_kernel(info_ref, x, xx, s1, w, wp, wm, high, low, high2, low2, whigh, wlow, held, sems):
    both = 2 * HALF
    copies = pull(info_ref, held, sems, [(x, 0, both, 0, 0), (xx, 0, both, 1, 0), (s1, 0, both, 2, 0), (s1, both, both, 3, 0)])
    start_all(copies)
    split_into(whigh, wlow, [w, wp, wm])
    wait_all(copies)
    dense(info_ref, held, [high, high2], [low, low2])


def ready(info, sources, weights):
    columns = weights[0].shape[1]
    return pl.pallas_call(
        ready_kernel,
        out_shape=[pltpu.VMEM((ROWS, DEEP), bf16)] * 4 + [pltpu.VMEM((384, columns), bf16)] * 2,
        in_specs=[pl.BlockSpec(memory_space=pltpu.SMEM)] + [ANYWHERE] * 3 + [WHOLE] * 3,
        out_specs=[WHOLE] * 6,
        scratch_shapes=[pltpu.VMEM((8, ROWS, 128), f32), pltpu.SemaphoreType.DMA((4,))],
        compiler_params=pltpu.CompilerParams(vmem_limit_bytes=READY * MIB),
        cost_estimate=pl.CostEstimate(flops=4 * ROWS * DEEP, bytes_accessed=10 * MIB, transcendentals=0),
        name="ready",
    )(info, *sources, *weights)


def early_kernel(info_ref, s2, xp, xxp, xm, xxm, w2, high, low, whigh3, wlow3,
                 part_ref, ahigh_ref, alow_ref, whigh, wlow, held, bhigh, blow, sems):
    both = 2 * HALF
    copies = [
        pull(info_ref, held.at[j], sems.at[j], [
            (near_ref, 0, both, 0, 0), (far_ref, 0, both, 1, 0), (s2, (2 * j + 2) * both, both, 2, 0), (s2, (2 * j + 3) * both, both, 3, 0)
        ])
        for j, (near_ref, far_ref) in enumerate(((xp, xxp), (xm, xxm)))
    ]
    start_all(copies[0] + copies[1])
    whigh[0:384] = whigh3[...]
    wlow[0:384] = wlow3[...]
    split_into(whigh, wlow, [w2], 3)
    for j in range(3):
        if j:
            wait_all(copies[j - 1])
            dense(info_ref, held.at[j - 1], [bhigh.at[j - 1], ahigh_ref.at[j - 1]], [blow.at[j - 1], alow_ref.at[j - 1]])
        h, l = (high, low) if j == 0 else (bhigh.at[j - 1], blow.at[j - 1])
        for n in range(0, part_ref.shape[2], 256):
            part_ref[j, :, n : n + 256] = three(h[...], l[...], whigh[:, n : n + 256], wlow[:, n : n + 256])


def early(info, sources, w2, made):
    columns = w2.shape[1]
    return pl.pallas_call(
        early_kernel,
        out_shape=[
            pltpu.VMEM((3, ROWS, columns), f32),
            pltpu.VMEM((2, ROWS, DEEP), bf16),
            pltpu.VMEM((2, ROWS, DEEP), bf16),
            pltpu.VMEM((DEEP, columns), bf16),
            pltpu.VMEM((DEEP, columns), bf16),
        ],
        in_specs=[pl.BlockSpec(memory_space=pltpu.SMEM)] + [ANYWHERE] * 5 + [WHOLE] * 5,
        out_specs=[WHOLE] * 5,
        scratch_shapes=[
            pltpu.VMEM((2, 8, ROWS, 128), f32),
            pltpu.VMEM((2, ROWS, DEEP), bf16),
            pltpu.VMEM((2, ROWS, DEEP), bf16),
            pltpu.SemaphoreType.DMA((2, 4)),
        ],
        compiler_params=pltpu.CompilerParams(vmem_limit_bytes=EARLY * MIB),
        cost_estimate=pl.CostEstimate(flops=18 * ROWS * DEEP * columns, bytes_accessed=20 * MIB, transcendentals=0),
        name="early",
    )(info, *sources, w2, *(near(v) for v in made))


def finish(out_ref, rgap_ref, cgap_ref, n, total):
    tall = rgap_ref[...].reshape(-1, 128)
    for m in range(0, 256, 128):
        gap = tall + cgap_ref[:, n + m : n + m + 128]
        out_ref[:, 0, :, n + m : n + m + 128] = (total[:, m : m + 128] / gap).reshape(-1, 8, 128)


def late_kernel(info_ref, part_ref, high2, low2, ahigh_ref, alow_ref, wx, wxp, wxm, wx2, rgap_ref, cgap_ref,
                out_ref, whigh2, wlow2):
    chunk = pl.program_id(0)

    @pl.when(chunk == 0)
    def _():
        split_into(whigh2, wlow2, [wx, wxp, wxm, wx2])

    def work(h, l):
        for n in range(0, whigh2.shape[1], 256):
            cut = slice(n, n + 256)
            finish(out_ref, rgap_ref, cgap_ref, n, part_ref[chunk, :, cut] + three(h[...], l[...], whigh2[:, cut], wlow2[:, cut]))

    pl.when(chunk == 0)(lambda: work(high2, low2))
    pl.when(chunk > 0)(lambda: work(ahigh_ref.at[chunk - 1], alow_ref.at[chunk - 1]))


def late(info, part, own, others, weights, rgap, cgap, virtuals):
    columns = weights[0].shape[1]
    rows = lambda *shape: pl.BlockSpec((virtuals, 1, 8) + shape, lambda c, i: (0, i[4 + c], 0, 0))
    return pl.pallas_call(
        late_kernel,
        out_shape=[jax.ShapeDtypeStruct((virtuals, 4, 8, columns), f32)] + [pltpu.VMEM((DEEP, columns), bf16)] * 2,
        grid_spec=pltpu.PrefetchScalarGridSpec(
            num_scalar_prefetch=1,
            grid=(3,),
            in_specs=[WHOLE] * 9 + [rows(128), WHOLE],
            out_specs=[rows(columns), WHOLE, WHOLE],
        ),
        compiler_params=pltpu.CompilerParams(vmem_limit_bytes=LATE * MIB),
        cost_estimate=pl.CostEstimate(flops=18 * ROWS * DEEP * columns, bytes_accessed=24 * MIB, transcendentals=0),
        name="late",
    )(info, *(near(v) for v in (part, *own, *others)), *weights, rgap, cgap)


def last_kernel(info_ref, rest_ref, up, down, s3, whigh, wlow, whigh2, wlow2, rgap_ref, cgap_ref,
                out_ref, held, *scratch):
    *scratch, sems = scratch
    high, low, high2, low2 = (scratch[n : n + 2] for n in range(0, 8, 2))
    del rest_ref
    step = pl.program_id(0)
    pieces = []
    for ref, base, slot in ((up, 0, 0), (down, 0, 0), (s3, 0, 2), (s3, 2 * HALF, 2)):
        offset = HALF * (len(pieces) // 2 % 2)
        pieces += [(ref, base, HALF, slot, offset), (ref, base + HALF, HALF, slot + 1, offset)]
    copies = pull(info_ref, held, sems, pieces)

    half = out_ref.shape[0]

    def work(h):
        for n in range(0, whigh.shape[1], 256):
            cut = slice(n, n + 256)
            total = three(high[h][...], low[h][...], whigh[:, cut], wlow[:, cut])
            total += three(high2[h][...], low2[h][...], whigh2[:, cut], wlow2[:, cut])
            finish(out_ref, rgap_ref, cgap_ref, n, total)

    def gather(h):
        dense(info_ref, held, [high[h], high2[h]], [low[h], low2[h]], range(h * half, h * half + half))

    @pl.when(step == 0)
    def _():
        start_all(copies)
        wait_all(copies)
        gather(0)
        gather(1)
        work(0)

    @pl.when(step == 1)
    def _():
        work(1)


def last(info, rest, sources, weights, rgap, cgap, virtuals):
    columns = weights[0].shape[1]
    steps = 2
    rows = lambda *shape: pl.BlockSpec((virtuals // steps, 1, 8) + shape, lambda c, i: (c, i[7], 0, 0))
    return pl.pallas_call(
        last_kernel,
        out_shape=jax.ShapeDtypeStruct((virtuals, 4, 8, columns), f32),
        grid_spec=pltpu.PrefetchScalarGridSpec(
            num_scalar_prefetch=1,
            grid=(steps,),
            in_specs=[APART] + [ANYWHERE] * 3 + [WHOLE] * 4 + [rows(128), WHOLE],
            out_specs=rows(columns),
            scratch_shapes=[pltpu.VMEM((8, ROWS, 128), f32)]
            + [pltpu.VMEM((ROWS // steps, DEEP), bf16)] * 8
            + [pltpu.SemaphoreType.DMA((8,))],
        ),
        input_output_aliases={1: 0},
        compiler_params=pltpu.CompilerParams(vmem_limit_bytes=LAST * MIB),
        cost_estimate=pl.CostEstimate(flops=12 * ROWS * DEEP * columns, bytes_accessed=8 * MIB, transcendentals=0),
        name="last",
    )(info, rest, *sources, *(near(v) for v in weights), rgap, cgap)


def body(amplitudes, integrals, occ_energy, vir_energy):
    virtuals, own = amplitudes.shape[:2]
    depth = amplitudes.shape[2] * amplitudes.shape[3]
    columns = integrals.shape[1]
    y, xl, core, xh, z = (lax.axis_index(a) for a in AXES)

    info = jnp.stack(
        [xl * 2 + core, (1 - xl) * 2 + core, xl * 2 + 1 - core, (1 - xl) * 2 + 1 - core]
        + [y, (y + 3) % 4, (y + 1) % 4, (y + 2) % 4]
        + [z, (z + 3) % 4, (z + 1) % 4, (z + 2) % 4]
        + [xh, 1 - xh]
    ).astype(jnp.int32)
    gap = vir_energy[:, None] - occ_energy[None, :]
    row_gap = lax.dynamic_slice_in_dim(gap, (xh * 4 + z) * virtuals, virtuals)
    rgap = jnp.broadcast_to(row_gap.reshape(virtuals, 4, 8, 1), (virtuals, 4, 8, 128))
    start = ((y * 2 + xl) * 2 + core) * columns
    cgap = lax.dynamic_slice_in_dim(gap.reshape(-1), start, columns).reshape(1, columns)

    join = lambda *values: jnp.concatenate(values, axis=1)
    x = turn(amplitudes.transpose(1, 2, 3, 0).reshape(own, depth, virtuals))
    w = integrals

    wp, wm = hop(w, z=1), hop(w, z=3)
    xp, xm, xx = hop(x, y=1), hop(x, y=3), hop(x, xl=1)
    xx, info, rgap, cgap = lax.optimization_barrier((xx, info, rgap, cgap))
    xxp, xxm = hop(xx, y=1), hop(xx, y=3)
    w2, wx = hop(after(w, wp, wm, xp, xm), z=2), hop(after(w, xx), xh=1)
    wx, xxp, xxm = lax.optimization_barrier((wx, xxp, xxm))
    wx, w2, xxp, xxm = lax.optimization_barrier((wx, w2, xxp, xxm))
    s2 = hop(join(x, xx, xp, xxp, xm, xxm), core=1)
    up = hop(join(xp[:, :HALF], xxp[:, :HALF]), y=1)
    down = hop(join(xm[:, HALF:], xxm[:, HALF:]), y=3)
    wxp, wxm, wx2 = hop(wx, z=1), hop(wx, z=3), hop(w2, xh=1)

    high, low, high2, low2, whigh, wlow = ready(info, [x, xx, s2], [w, wp, wm])
    part, ahigh, alow, whigh, wlow = early(info, [s2, xp, xxp, xm, xxm], w2, [high, low, whigh, wlow])
    up, down, wxp, wxm, wx2, wlow = lax.optimization_barrier((up, down, wxp, wxm, wx2, wlow))
    s3 = hop(join(up, down), core=1)
    out, whigh2, wlow2 = late(info, part, [high2, low2], [ahigh, alow], [wx, wxp, wxm, wx2], rgap, cgap, virtuals)
    out = last(info, out, [up, down, s3], [whigh, wlow, whigh2, wlow2], rgap, cgap, virtuals)
    return out.reshape(virtuals * 32, columns)


def solution(mesh):
    fine = Mesh(mesh.devices.reshape(SIZES), AXES)
    in_specs = (P(COL, ROW, None, None), P(COL, ROW), P(), P())
    return jax.shard_map(body, mesh=fine, in_specs=in_specs, out_specs=P(COL, ROW), check_vma=False)
```

```python
import functools

import jax
import jax.numpy as jnp
import numpy as np
from jax import lax
from jax.experimental import pallas as pl
from jax.experimental.pallas import tpu as pltpu
from jax.sharding import Mesh, PartitionSpec as P

ROW = ("y", "xl", "core")
COL = ("xh", "z")
AXES = ROW + COL
SIZES = (4, 2, 2, 2, 4)
f32, bf16 = jnp.float32, jnp.bfloat16
MIB = 1 << 20
READY, EARLY, LATE, LAST = 20, 24, 24, 24
TURN_FLOPS = 1 << 20
HALF = 64


def hop(value, **move):
    pairs = []
    for source in range(int(np.prod(SIZES))):
        place = list(np.unravel_index(source, SIZES))
        for axis, step in move.items():
            k = AXES.index(axis)
            place[k] = (place[k] + step) % SIZES[k]
        pairs.append((source, int(np.ravel_multi_index(place, SIZES))))
    return lax.ppermute(value, AXES, pairs)


def after(value, *needed):
    return lax.optimization_barrier((value,) + needed)[0]


def split(value):
    high = value.astype(bf16)
    return high, (value - high.astype(f32)).astype(bf16)


def turn_kernel(amp_ref, out_ref):
    for n in range(out_ref.shape[0]):
        lanes = slice(n * 128, n * 128 + 128)
        both = jnp.concatenate([amp_ref[0, lanes], amp_ref[1, lanes]], axis=1)
        out_ref[n] = both.T


def turn(amp):
    two, depth, width = amp.shape
    steps = 2
    return pl.pallas_call(
        turn_kernel,
        out_shape=jax.ShapeDtypeStruct((depth // 128, two * width, 128), f32),
        grid=(steps,),
        in_specs=[pl.BlockSpec((two, depth // steps, width), lambda s: (0, s, 0))],
        out_specs=pl.BlockSpec((depth // 128 // steps, two * width, 128), lambda s: (s, 0, 0)),
        name="turn",
    )(amp)


def dense(info_ref, held, high_refs, low_refs, rows=range(64)):
    width = held.shape[1] // 8
    for h in range(2):
        base = info_ref[12 + h] * 4
        for k in range(4):
            block = held.at[base + info_ref[8 + k]]
            for a in range(rows.start, rows.stop, 2):
                value = jnp.concatenate([block[pl.ds(a + b, 8, stride=width), :] for b in range(2)], axis=0)
                high, low = split(value)
                row = (a - rows.start) * 8
                high_refs[h][row : row + 16, k * 128 : k * 128 + 128] = high
                low_refs[h][row : row + 16, k * 128 : k * 128 + 128] = low


def three(high, low, whigh, wlow):
    total = jnp.dot(high, whigh, preferred_element_type=f32)
    total += jnp.dot(high, wlow, preferred_element_type=f32)
    return total + jnp.dot(low, whigh, preferred_element_type=f32)


def pull(info_ref, held, sems, pieces):
    copies = []
    for n, (ref, start, rows, slot, offset) in enumerate(pieces):
        row = pl.multiple_of(info_ref[slot] * (2 * HALF) + offset, 8)
        copies.append(pltpu.make_async_copy(ref.at[:, pl.ds(start, rows)], held.at[:, pl.ds(row, rows)], sems.at[n]))
    return copies


def start_all(copies):
    for copy in copies:
        copy.start()


def wait_all(copies):
    for copy in copies:
        copy.wait()


def split_into(high_ref, low_ref, pieces, first=0):
    for n, ref in enumerate(pieces):
        row = (first + n) * 128
        high_ref[row : row + 128], low_ref[row : row + 128] = split(ref[...])


WHOLE = pl.BlockSpec(memory_space=pltpu.VMEM)
APART = pl.BlockSpec(memory_space=pltpu.HBM)
ANYWHERE = pl.BlockSpec(memory_space=pl.ANY)
ROWS = 8 * HALF
DEEP = 512
near = lambda value: pltpu.with_memory_space_constraint(value, pltpu.VMEM)


def ready_kernel(info_ref, x, xx, s1, w, wp, wm, high, low, high2, low2, whigh, wlow, held, sems):
    both = 2 * HALF
    copies = pull(info_ref, held, sems, [(x, 0, both, 0, 0), (xx, 0, both, 1, 0), (s1, 0, both, 2, 0), (s1, both, both, 3, 0)])
    start_all(copies)
    split_into(whigh, wlow, [w, wp, wm])
    wait_all(copies)
    dense(info_ref, held, [high, high2], [low, low2])


def ready(info, sources, weights):
    columns = weights[0].shape[1]
    return pl.pallas_call(
        ready_kernel,
        out_shape=[pltpu.VMEM((ROWS, DEEP), bf16)] * 4 + [pltpu.VMEM((384, columns), bf16)] * 2,
        in_specs=[pl.BlockSpec(memory_space=pltpu.SMEM)] + [ANYWHERE] * 3 + [WHOLE] * 3,
        out_specs=[WHOLE] * 6,
        scratch_shapes=[pltpu.VMEM((8, ROWS, 128), f32), pltpu.SemaphoreType.DMA((4,))],
        compiler_params=pltpu.CompilerParams(vmem_limit_bytes=READY * MIB),
        cost_estimate=pl.CostEstimate(flops=4 * ROWS * DEEP, bytes_accessed=10 * MIB, transcendentals=0),
        name="ready",
    )(info, *sources, *weights)


def early_kernel(info_ref, s2, xp, xxp, xm, xxm, w2, high, low, whigh3, wlow3,
                 part_ref, ahigh_ref, alow_ref, whigh, wlow, held, bhigh, blow, sems):
    both = 2 * HALF
    copies = [
        pull(info_ref, held.at[j], sems.at[j], [
            (near_ref, 0, both, 0, 0), (far_ref, 0, both, 1, 0), (s2, (2 * j + 2) * both, both, 2, 0), (s2, (2 * j + 3) * both, both, 3, 0)
        ])
        for j, (near_ref, far_ref) in enumerate(((xp, xxp), (xm, xxm)))
    ]
    start_all(copies[0] + copies[1])
    whigh[0:384] = whigh3[...]
    wlow[0:384] = wlow3[...]
    split_into(whigh, wlow, [w2], 3)
    for j in range(3):
        if j:
            wait_all(copies[j - 1])
            dense(info_ref, held.at[j - 1], [bhigh.at[j - 1], ahigh_ref.at[j - 1]], [blow.at[j - 1], alow_ref.at[j - 1]])
        h, l = (high, low) if j == 0 else (bhigh.at[j - 1], blow.at[j - 1])
        for n in range(0, part_ref.shape[2], 256):
            part_ref[j, :, n : n + 256] = three(h[...], l[...], whigh[:, n : n + 256], wlow[:, n : n + 256])


def early(info, sources, w2, made):
    columns = w2.shape[1]
    return pl.pallas_call(
        early_kernel,
        out_shape=[
            pltpu.VMEM((3, ROWS, columns), f32),
            pltpu.VMEM((2, ROWS, DEEP), bf16),
            pltpu.VMEM((2, ROWS, DEEP), bf16),
            pltpu.VMEM((DEEP, columns), bf16),
            pltpu.VMEM((DEEP, columns), bf16),
        ],
        in_specs=[pl.BlockSpec(memory_space=pltpu.SMEM)] + [ANYWHERE] * 5 + [WHOLE] * 5,
        out_specs=[WHOLE] * 5,
        scratch_shapes=[
            pltpu.VMEM((2, 8, ROWS, 128), f32),
            pltpu.VMEM((2, ROWS, DEEP), bf16),
            pltpu.VMEM((2, ROWS, DEEP), bf16),
            pltpu.SemaphoreType.DMA((2, 4)),
        ],
        compiler_params=pltpu.CompilerParams(vmem_limit_bytes=EARLY * MIB),
        cost_estimate=pl.CostEstimate(flops=18 * ROWS * DEEP * columns, bytes_accessed=20 * MIB, transcendentals=0),
        name="early",
    )(info, *sources, w2, *(near(v) for v in made))


def finish(out_ref, rgap_ref, cgap_ref, n, total):
    tall = rgap_ref[...].reshape(-1, 128)
    for m in range(0, 256, 128):
        gap = tall + cgap_ref[:, n + m : n + m + 128]
        out_ref[:, 0, :, n + m : n + m + 128] = (total[:, m : m + 128] / gap).reshape(-1, 8, 128)


def late_kernel(info_ref, part_ref, high2, low2, ahigh_ref, alow_ref, wx, wxp, wxm, wx2, rgap_ref, cgap_ref,
                out_ref, whigh2, wlow2):
    chunk = pl.program_id(0)

    @pl.when(chunk == 0)
    def _():
        split_into(whigh2, wlow2, [wx, wxp, wxm, wx2])

    def work(h, l):
        for n in range(0, whigh2.shape[1], 256):
            cut = slice(n, n + 256)
            finish(out_ref, rgap_ref, cgap_ref, n, part_ref[chunk, :, cut] + three(h[...], l[...], whigh2[:, cut], wlow2[:, cut]))

    pl.when(chunk == 0)(lambda: work(high2, low2))
    pl.when(chunk > 0)(lambda: work(ahigh_ref.at[chunk - 1], alow_ref.at[chunk - 1]))


def late(info, part, own, others, weights, rgap, cgap, virtuals):
    columns = weights[0].shape[1]
    rows = lambda *shape: pl.BlockSpec((virtuals, 1, 8) + shape, lambda c, i: (0, i[4 + c], 0, 0))
    return pl.pallas_call(
        late_kernel,
        out_shape=[jax.ShapeDtypeStruct((virtuals, 4, 8, columns), f32)] + [pltpu.VMEM((DEEP, columns), bf16)] * 2,
        grid_spec=pltpu.PrefetchScalarGridSpec(
            num_scalar_prefetch=1,
            grid=(3,),
            in_specs=[WHOLE] * 9 + [rows(128), WHOLE],
            out_specs=[rows(columns), WHOLE, WHOLE],
        ),
        compiler_params=pltpu.CompilerParams(vmem_limit_bytes=LATE * MIB),
        cost_estimate=pl.CostEstimate(flops=18 * ROWS * DEEP * columns, bytes_accessed=24 * MIB, transcendentals=0),
        name="late",
    )(info, *(near(v) for v in (part, *own, *others)), *weights, rgap, cgap)


def last_kernel(info_ref, rest_ref, up, down, s3, whigh, wlow, whigh2, wlow2, rgap_ref, cgap_ref,
                out_ref, held, *scratch):
    *scratch, sems = scratch
    high, low, high2, low2 = (scratch[n : n + 2] for n in range(0, 8, 2))
    del rest_ref
    step = pl.program_id(0)
    pieces = []
    for ref, base, slot in ((up, 0, 0), (down, 0, 0), (s3, 0, 2), (s3, 2 * HALF, 2)):
        offset = HALF * (len(pieces) // 2 % 2)
        pieces += [(ref, base, HALF, slot, offset), (ref, base + HALF, HALF, slot + 1, offset)]
    copies = pull(info_ref, held, sems, pieces)

    half = out_ref.shape[0]

    def work(h):
        for n in range(0, whigh.shape[1], 256):
            cut = slice(n, n + 256)
            total = three(high[h][...], low[h][...], whigh[:, cut], wlow[:, cut])
            total += three(high2[h][...], low2[h][...], whigh2[:, cut], wlow2[:, cut])
            finish(out_ref, rgap_ref, cgap_ref, n, total)

    def gather(h):
        dense(info_ref, held, [high[h], high2[h]], [low[h], low2[h]], range(h * half, h * half + half))

    @pl.when(step == 0)
    def _():
        start_all(copies)
        wait_all(copies)
        gather(0)
        gather(1)
        work(0)

    @pl.when(step == 1)
    def _():
        work(1)


def last(info, rest, sources, weights, rgap, cgap, virtuals):
    columns = weights[0].shape[1]
    steps = 2
    rows = lambda *shape: pl.BlockSpec((virtuals // steps, 1, 8) + shape, lambda c, i: (c, i[7], 0, 0))
    return pl.pallas_call(
        last_kernel,
        out_shape=jax.ShapeDtypeStruct((virtuals, 4, 8, columns), f32),
        grid_spec=pltpu.PrefetchScalarGridSpec(
            num_scalar_prefetch=1,
            grid=(steps,),
            in_specs=[APART] + [ANYWHERE] * 3 + [WHOLE] * 4 + [rows(128), WHOLE],
            out_specs=rows(columns),
            scratch_shapes=[pltpu.VMEM((8, ROWS, 128), f32)]
            + [pltpu.VMEM((ROWS // steps, DEEP), bf16)] * 8
            + [pltpu.SemaphoreType.DMA((8,))],
        ),
        input_output_aliases={1: 0},
        compiler_params=pltpu.CompilerParams(vmem_limit_bytes=LAST * MIB),
        cost_estimate=pl.CostEstimate(flops=12 * ROWS * DEEP * columns, bytes_accessed=8 * MIB, transcendentals=0),
        name="last",
    )(info, rest, *sources, *(near(v) for v in weights), rgap, cgap)


def body(amplitudes, integrals, occ_energy, vir_energy):
    virtuals, own = amplitudes.shape[:2]
    depth = amplitudes.shape[2] * amplitudes.shape[3]
    columns = integrals.shape[1]
    y, xl, core, xh, z = (lax.axis_index(a) for a in AXES)

    info = jnp.stack(
        [xl * 2 + core, (1 - xl) * 2 + core, xl * 2 + 1 - core, (1 - xl) * 2 + 1 - core]
        + [y, (y + 3) % 4, (y + 1) % 4, (y + 2) % 4]
        + [z, (z + 3) % 4, (z + 1) % 4, (z + 2) % 4]
        + [xh, 1 - xh]
    ).astype(jnp.int32)
    gap = vir_energy[:, None] - occ_energy[None, :]
    row_gap = lax.dynamic_slice_in_dim(gap, (xh * 4 + z) * virtuals, virtuals)
    rgap = jnp.broadcast_to(row_gap.reshape(virtuals, 4, 8, 1), (virtuals, 4, 8, 128))
    start = ((y * 2 + xl) * 2 + core) * columns
    cgap = lax.dynamic_slice_in_dim(gap.reshape(-1), start, columns).reshape(1, columns)

    join = lambda *values: jnp.concatenate(values, axis=1)
    x = turn(amplitudes.transpose(1, 2, 3, 0).reshape(own, depth, virtuals))
    w = integrals

    wp, wm = hop(w, z=1), hop(w, z=3)
    xp, xm, xx = hop(x, y=1), hop(x, y=3), hop(x, xl=1)
    xx, info, rgap, cgap = lax.optimization_barrier((xx, info, rgap, cgap))
    xxp, xxm = hop(xx, y=1), hop(xx, y=3)
    w2, wx = hop(after(w, wp, wm, xp, xm), z=2), hop(after(w, xx), xh=1)
    wx, xxp, xxm = lax.optimization_barrier((wx, xxp, xxm))
    wx, w2, xxp, xxm = lax.optimization_barrier((wx, w2, xxp, xxm))
    s2 = hop(join(x, xx, xp, xxp, xm, xxm), core=1)
    up = hop(join(xp[:, :HALF], xxp[:, :HALF]), y=1)
    down = hop(join(xm[:, HALF:], xxm[:, HALF:]), y=3)
    wxp, wxm, wx2 = hop(wx, z=1), hop(wx, z=3), hop(w2, xh=1)

    high, low, high2, low2, whigh, wlow = ready(info, [x, xx, s2], [w, wp, wm])
    part, ahigh, alow, whigh, wlow = early(info, [s2, xp, xxp, xm, xxm], w2, [high, low, whigh, wlow])
    up, down, wxp, wxm, wx2, wlow = lax.optimization_barrier((up, down, wxp, wxm, wx2, wlow))
    s3 = hop(join(up, down), core=1)
    out, whigh2, wlow2 = late(info, part, [high2, low2], [ahigh, alow], [wx, wxp, wxm, wx2], rgap, cgap, virtuals)
    out = last(info, out, [up, down, s3], [whigh, wlow, whigh2, wlow2], rgap, cgap, virtuals)
    return out.reshape(virtuals * 32, columns)


def solution(mesh):
    fine = Mesh(mesh.devices.reshape(SIZES), AXES)
    in_specs = (P(COL, ROW, None, None), P(COL, ROW), P(), P())
    return jax.shard_map(body, mesh=fine, in_specs=in_specs, out_specs=P(COL, ROW), check_vma=False)
```
